256 devices in a mesh: tm: 64 (over y_hi, x, z), space: 4 (over y_lo, core).
Axes of the slice: x: 4, y: 4 (y_hi: 2, y_lo: 2; y = y_hi * 2 + y_lo), z: 8, core: 2. Of those that a mesh axis runs over, the one named last changes fastest.
Arguments:
- guess: float32 [64, 1024, 1024], P('tm', 'space'), may hold values from -2.5 to 2.5
- kappa: float32 [1024, 1024], P('space'), may hold values from 0.25 to 1
- rate: float32 [1024, 1024], P('space'), may hold values from 0.005 to 0.02
Outputs:
- c_points: float32 [64, 1024, 1024], P('tm', 'space')
- last_fine: float32 [64, 1024, 1024], P('tm', 'space')
The draws below stay inside these ranges and needn't reach their ends.
All inputs are finite; a program needn't handle non-finite values.
Results may differ from the reference program's by a relative error of at most 0.00002.
Values sent between devices are 32-bit elements; how exact they have to be, the bound alone decides.
No kernel may reach another device: no remote copies, remote signals or barrier semaphores. Data moves between devices by JAX's collectives and lax.ppermute only.
A program may use at most 64 MiB of HBM per device.

```python
import math
import jax
import jax.numpy as jnp

NY = 1024
STEPS = 4
GROUP = 4
SWEEPS = 2
NT = 64
NX = 1024


def level_of(key, dims, cuts, smallest, top_value):
    loudness, own = 1.0, jax.random.fold_in(key, 6)
    for axis_at, blocks in cuts:
        heights = jnp.exp(jax.random.uniform(jax.random.fold_in(own, axis_at), (blocks,), jnp.float32, smallest / len(cuts), top_value / len(cuts)))
        loudness = loudness * jnp.repeat(heights, dims[axis_at] // blocks).reshape([-1 if axis == axis_at else 1 for axis in range(len(dims))])
    return loudness


def bell_draw(own_key, extent, scale, most, cuts=(), kind=jnp.bfloat16):
    result = scale * jax.random.normal(own_key, extent, jnp.float32)
    if cuts:
        result = result * level_of(own_key, extent, cuts, -0.22, 0.18)
    return jnp.clip(result, -most, most).astype(kind)


def setup_inputs(seed: int = 0) -> dict:
    arg_keys = jax.random.split(jax.random.key(seed), 4)
    return {
        "guess": bell_draw(arg_keys[0], (NT, NX, NY), 0.5, 2.5, ((0, 64), (1, 4)), jnp.float32),
        "kappa": jnp.clip(jnp.exp(math.log(1.0) - 1.3862944 * jax.random.uniform(arg_keys[1], (NX, NY), jnp.float32) ** level_of(arg_keys[1], (NX, NY), ((0, 4),), -0.2, 0.2)), 0.25, 1.0),
        "rate": jnp.clip(jnp.exp(math.log(0.02) - 1.3862944 * jax.random.uniform(arg_keys[2], (NX, NY), jnp.float32) ** level_of(arg_keys[2], (NX, NY), ((0, 4),), -0.2, 0.2)), 0.005, 0.02),
    }


DIFFUSION = 0.05


def advance_padded(padded, kappa, rate, scale):
    centre = padded[..., 1:-1, 1:-1]
    laplace = padded[..., 2:, 1:-1] + padded[..., :-2, 1:-1] + padded[..., 1:-1, 2:] + padded[..., 1:-1, :-2] - 4.0 * centre
    return centre + scale * (DIFFUSION * kappa * laplace + rate * (centre - centre * centre * centre))


def advance(state, kappa, rate, scale):
    widths = [(0, 0)] * (state.ndim - 2) + [(1, 1), (1, 1)]
    return advance_padded(jnp.pad(state, widths), kappa, rate, scale)


def propagate(state, kappa, rate, count):
    for repeat in range(count):
        state = advance(state, kappa, rate, 1.0)
    return state


def reference(guess, kappa, rate):
    first = guess[:1]
    relaxed = jnp.concatenate([first, propagate(guess[:-1], kappa, rate, STEPS)], axis=0)
    earlier = relaxed[:-1]
    fine_image = propagate(earlier, kappa, rate, STEPS)
    coarse_image = advance(earlier, kappa, rate, float(STEPS))
    defect = jnp.concatenate([jnp.zeros_like(first), fine_image - coarse_image], axis=0)
    groups = NT // GROUP
    coarse = relaxed.reshape(groups, GROUP, NX, NY)
    defects = defect.reshape(groups, GROUP, NX, NY)
    for sweep_number in range(SWEEPS):
        for member in range(1, GROUP):
            coarse = coarse.at[:, member].set(advance(coarse[:, member - 1], kappa, rate, float(STEPS)) + defects[:, member])
        coarse = coarse.at[1:, 0].set(advance(coarse[:-1, GROUP - 1], kappa, rate, float(STEPS)) + defects[1:, 0])
    c_points = coarse.reshape(NT, NX, NY)
    last_fine = propagate(c_points, kappa, rate, STEPS - 1)
    return c_points, last_fine
```

```python
import functools

import jax
import jax.numpy as jnp
from jax import lax
from jax.experimental import pallas as pl
from jax.experimental.pallas import tpu as pltpu
from jax.sharding import PartitionSpec as P

STEPS = 4
GROUP = 4
DIFFUSION = 0.05
RING = 8
HALO = 24
LANES = 128
FRAME = 16
EDGE = 11
PACK = 64
TAIL = 4
GUARD = 8


def lane_index():
    return lax.broadcasted_iota(jnp.int32, (8, LANES), 1)


def neighbour_sum(tiles, up, down):
    lane = lane_index()
    count = len(tiles)
    right_turned = [pltpu.roll(t, 1, 1) for t in tiles]
    left_turned = [pltpu.roll(t, LANES - 1, 1) for t in tiles]
    sums = []
    for i in range(count):
        left = jnp.where(lane == 0, right_turned[i - 1], right_turned[i])
        right = jnp.where(lane == LANES - 1, left_turned[(i + 1) % count], left_turned[i])
        sums.append((up[i] + down[i]) + (left + right))
    return sums


def stepped(ref, at, row, coefs):
    count = len(coefs)
    tiles = [ref[at + (i, pl.ds(row, 8), slice(None))] for i in range(count)]
    up = [ref[at + (i, pl.ds(row - 1, 8), slice(None))] for i in range(count)]
    down = [ref[at + (i, pl.ds(row + 1, 8), slice(None))] for i in range(count)]
    sums = neighbour_sum(tiles, up, down)
    out = [k * s + c * (m - r * (c * c)) for c, s, (k, r, m) in zip(tiles, sums, coefs)]
    return out, tiles


def rows_of(ref, kinds, count, row):
    return [tuple(ref[k, i, pl.ds(row, 8), :] for k in kinds) for i in range(count)]


def each_block(first, last, body, unroll=1):
    def trip(i, carry):
        body(pl.multiple_of(first + 8 * i, 8))
        return carry

    lax.fori_loop(0, (last - first) // 8, trip, 0, unroll=unroll)


def relax_kernel(g_ref, k_ref, r_ref, lo_ref, hi_ref, packed_ref, own_ref, u_ref, w_ref, c_ref):
    rows, columns = g_ref.shape
    tiles = columns // LANES
    ext = rows + 2 * HALO
    top = GUARD + HALO
    zero8 = jnp.zeros((GUARD, LANES), jnp.float32)

    def fill(put, body_ref, part):
        for t in range(tiles):
            cols = slice(t * LANES, (t + 1) * LANES)
            put(t, GUARD, HALO, lambda a, n: lo_ref[part, pl.ds(a, n), cols])
            put(t, top, rows, lambda a, n: body_ref[pl.ds(a, n), cols])
            put(t, top + rows, HALO, lambda a, n: hi_ref[part, pl.ds(a, n), cols])

    def put_u(t, at, n, load):
        u_ref[t, at : at + n, :] = load(0, n)

    def put_k(t, at, n, load):
        c_ref[0, t, at : at + n, :] = DIFFUSION * load(0, n)

    def put_r(t, at, n, load):
        rate = load(0, n)
        c_ref[1, t, at : at + n, :] = rate
        c_ref[2, t, at : at + n, :] = 1.0 - 4.0 * c_ref[0, t, at : at + n, :] + rate

    fill(put_u, g_ref, 0)
    fill(put_k, k_ref, 1)
    fill(put_r, r_ref, 2)
    pad = jnp.zeros((ext + 2 * GUARD, LANES), jnp.float32)
    u_ref[tiles] = pad
    w_ref[tiles] = pad
    for kind in range(2):
        c_ref[kind, tiles] = pad
    c_ref[2, tiles] = pad + 1.0
    for t in range(tiles):
        for ref in (u_ref, w_ref):
            ref[t, 0:GUARD, :] = zero8
            ref[t, GUARD + ext : ext + 2 * GUARD, :] = zero8

    def march(src, dst, first, last):
        def body(row):
            out, _ = stepped(src, (), row, rows_of(c_ref, (0, 1, 2), tiles + 1, row))
            for t in range(tiles):
                dst[t, pl.ds(row, 8), :] = out[t]

        each_block(first, last, body)

    march(u_ref, w_ref, GUARD, GUARD + ext)
    march(w_ref, u_ref, GUARD, GUARD + ext)
    march(u_ref, w_ref, GUARD + 8, GUARD + ext - 8)
    march(w_ref, u_ref, GUARD + 8, GUARD + ext - 8)

    frame = rows + 2 * FRAME
    base = top - FRAME
    lane = lane_index()
    for c in range(RING):
        packed_ref[c, 0:frame, :] = u_ref[c, base : base + frame, :]
        after, before = c + 1, (c - 1) % (tiles + 1)
        for block in range(PACK // 8):
            acc = jnp.zeros((8, LANES), jnp.float32)
            for part in range(pl.cdiv(frame, PACK)):
                at = part * PACK + block * 8
                if at < frame:
                    edge = jnp.where(
                        lane < LANES // 2,
                        u_ref[after, base + at : base + at + 8, :],
                        u_ref[before, base + at : base + at + 8, :],
                    )
                    begin = 2 * EDGE * part
                    turned = pltpu.roll(edge, EDGE + begin, 1)
                    acc = jnp.where((lane >= begin) & (lane < begin + 2 * EDGE), turned, acc)
            packed_ref[c, frame + 8 * block : frame + 8 * block + 8, :] = acc

    mine = (lax.axis_index("tm") + 1) % RING
    after, before = mine + 1, lax.rem(mine + tiles, tiles + 1)
    near = (lane < EDGE) | (lane >= LANES - EDGE)
    for kind in range(3):
        own_ref[kind, 0, 0:GUARD, :] = zero8
        own_ref[kind, 1, 0:GUARD, :] = zero8
        own_ref[kind, 0, GUARD + frame :, :] = zero8
        own_ref[kind, 1, GUARD + frame :, :] = zero8

        def body(row, kind=kind):
            src = row + base - GUARD
            own_ref[kind, 0, pl.ds(row, 8), :] = c_ref[kind, mine, pl.ds(src, 8), :]
            edge = jnp.where(
                lane < LANES // 2,
                c_ref[kind, after, pl.ds(src, 8), :],
                c_ref[kind, before, pl.ds(src, 8), :],
            )
            far = 1.0 if kind == 2 else 0.0
            own_ref[kind, 1, pl.ds(row, 8), :] = jnp.where(near, edge, far)

        each_block(GUARD, GUARD + frame, body)


def unpack(src_ref, at, dst_ref, to, frame):
    zero8 = jnp.zeros((GUARD, LANES), jnp.float32)
    for i in range(2):
        dst_ref[to, i, 0:GUARD, :] = zero8
        dst_ref[to, i, GUARD + frame : frame + 2 * GUARD, :] = zero8
    dst_ref[to, 0, GUARD : GUARD + frame, :] = src_ref[at + (slice(0, frame),)]
    for part in range(pl.cdiv(frame, PACK)):
        count = min(PACK, frame - part * PACK)
        block = src_ref[at + (slice(frame, frame + count),)]
        turned = pltpu.roll(block, (-(2 * EDGE * part + EDGE)) % LANES, 1)
        dst_ref[to, 1, GUARD + part * PACK : GUARD + part * PACK + count, :] = turned


def pack(src_ref, at, dst_ref, frame):
    lane = lane_index()
    dst_ref[0:frame, :] = src_ref[at, 0, GUARD : GUARD + frame, :]
    for block in range(PACK // 8):
        acc = jnp.zeros((8, LANES), jnp.float32)
        for part in range(pl.cdiv(frame, PACK)):
            row = part * PACK + block * 8
            if row < frame:
                begin = 2 * EDGE * part
                edge = src_ref[at, 1, GUARD + row : GUARD + row + 8, :]
                turned = pltpu.roll(edge, EDGE + begin, 1)
                acc = jnp.where((lane >= begin) & (lane < begin + 2 * EDGE), turned, acc)
        dst_ref[frame + 8 * block : frame + 8 * block + 8, :] = acc


def coarse_coefs(own_ref, row):
    fine = rows_of(own_ref, (0, 1, 2), 2, row)
    return [(STEPS * k, STEPS * r, STEPS * m - (STEPS - 1.0)) for k, r, m in fine]


def defects(in_ref, first, own_ref, x_ref, y_ref, d_ref, frame):
    for f in range(GROUP):
        unpack(in_ref, (first + f,), x_ref, f, frame)
        zero8 = jnp.zeros((GUARD, LANES), jnp.float32)
        for i in range(2):
            y_ref[f, i, 0:GUARD, :] = zero8
            y_ref[f, i, GUARD + frame : frame + 2 * GUARD, :] = zero8
    for step in range(STEPS):
        src, dst = (x_ref, y_ref) if step % 2 == 0 else (y_ref, x_ref)

        def body(row, step=step, src=src, dst=dst):
            coefs = rows_of(own_ref, (0, 1, 2), 2, row)
            for f in range(GROUP):
                out, old = stepped(src, (f,), row, coefs)
                for i in range(2):
                    dst[f, i, pl.ds(row, 8), :] = out[i]
                    if step == 0:
                        d_ref[f, i, pl.ds(row, 8), :] = STEPS * out[i] - (STEPS - 1.0) * old[i]
                    if step == STEPS - 1:
                        d_ref[f, i, pl.ds(row, 8), :] = out[i] - d_ref[f, i, pl.ds(row, 8), :]

        each_block(GUARD, GUARD + frame, body)


def chain_step(src_ref, at, dst_ref, to, own_ref, d_ref, which, frame, also=None):
    def body(row):
        out, _ = stepped(src_ref, (at,), row, coarse_coefs(own_ref, row))
        for i in range(2):
            value = out[i] + d_ref[which, i, pl.ds(row, 8), :]
            dst_ref[to, i, pl.ds(row, 8), :] = value

    each_block(GUARD, GUARD + frame, body)


def later_kernel(in_ref, own_ref, d_ref, sent_ref, x_ref, y_ref):
    frame = in_ref.shape[1] - PACK
    defects(in_ref, GROUP, own_ref, x_ref, y_ref, d_ref, frame)
    chain_step(x_ref, 0, y_ref, 0, own_ref, d_ref, 1, frame)
    chain_step(y_ref, 0, x_ref, 0, own_ref, d_ref, 2, frame)
    chain_step(x_ref, 0, y_ref, 0, own_ref, d_ref, 3, frame)
    pack(y_ref, 0, sent_ref, frame)


def emit(src_ref, at, out_ref, field, strip):
    z = lax.axis_index("tm") % RING
    slot = (field + 1 - z + RING) % RING
    begin = GUARD + FRAME - TAIL
    out_ref[slot] = src_ref[at, 0, begin : begin + strip + 2 * TAIL, :]


def earlier_kernel(in_ref, own_ref, later_d_ref, d_ref, one_ref, out_ref, x_ref, y_ref):
    frame = in_ref.shape[1] - PACK
    strip = frame - 2 * FRAME
    defects(in_ref, 0, own_ref, x_ref, y_ref, d_ref, frame)
    unpack(in_ref, (1,), one_ref, 0, frame)

    @pl.when(lax.axis_index("tm") + 1 < RING)
    def _():
        x_ref[0] = one_ref[0]

    @pl.when(lax.axis_index("tm") == lax.axis_size("tm") - 1)
    def _():
        x_ref[0] = one_ref[0]

    chain_step(x_ref, 0, y_ref, 0, own_ref, d_ref, 1, frame)
    chain_step(y_ref, 0, x_ref, 0, own_ref, d_ref, 2, frame)
    chain_step(x_ref, 0, y_ref, 0, own_ref, d_ref, 3, frame)
    for i in range(GROUP):
        src, dst = (y_ref, x_ref) if i % 2 == 0 else (x_ref, y_ref)
        chain_step(src, 0, dst, 0, own_ref, later_d_ref, i, frame)
        emit(dst, 0, out_ref, GROUP + i, strip)


def last_kernel(got_ref, own_ref, d_ref, one_ref, half_ref, out_ref, x_ref, y_ref):
    frame = got_ref.shape[0] - PACK
    strip = frame - 2 * FRAME
    out_ref[...] = half_ref[...]
    unpack(got_ref, (), x_ref, 0, frame)
    zero8 = jnp.zeros((GUARD, LANES), jnp.float32)
    for i in range(2):
        y_ref[0, i, 0:GUARD, :] = zero8
        y_ref[0, i, GUARD + frame : frame + 2 * GUARD, :] = zero8
    for i in range(GROUP):
        src, dst = (x_ref, y_ref) if i % 2 == 0 else (y_ref, x_ref)
        chain_step(src, 0, dst, 0, own_ref, d_ref, i, frame)
        if i == 0:
            member = (lax.axis_index("tm") + 1) % lax.axis_size("tm")

            @pl.when(member < RING)
            def _():
                dst[0] = one_ref[0]

        emit(dst, 0, out_ref, i, strip)


def fine_kernel(g_ref, k_ref, r_ref, lo_ref, hi_ref, *refs):
    blocks, (points_ref, last_ref, u_ref, w_ref, c_ref) = refs[:RING], refs[RING:]
    rows, columns = g_ref.shape
    tiles = columns // LANES
    tall = rows + 2 * TAIL
    zero8 = jnp.zeros((GUARD, LANES), jnp.float32)
    me = lax.axis_index("tm")
    for ref in (u_ref, w_ref):
        ref[tiles] = jnp.zeros((tall + 2 * GUARD, LANES), jnp.float32)
        for t in range(tiles):
            ref[t, 0:GUARD, :] = zero8
            ref[t, GUARD + tall : tall + 2 * GUARD, :] = zero8
    inner = GUARD + TAIL

    def spread(part, body_ref, store):
        for t in range(tiles):
            cols = slice(t * LANES, (t + 1) * LANES)
            store(t, GUARD, TAIL, lo_ref[part, HALO - TAIL : HALO, cols])
            store(t, inner, rows, body_ref[:, cols])
            store(t, inner + rows, TAIL, hi_ref[part, 0:TAIL, cols])

    def store_k(t, at, n, value):
        c_ref[0, t, at : at + n, :] = DIFFUSION * value

    def store_r(t, at, n, value):
        c_ref[1, t, at : at + n, :] = value
        c_ref[2, t, at : at + n, :] = 1.0 - 4.0 * c_ref[0, t, at : at + n, :] + value

    def store_u(t, at, n, value):
        u_ref[t, at : at + n, :] = value

    spread(1, k_ref, store_k)
    spread(2, r_ref, store_r)
    pad = jnp.zeros((tall + 2 * GUARD, LANES), jnp.float32)
    c_ref[0, tiles] = pad
    c_ref[1, tiles] = pad
    c_ref[2, tiles] = pad + 1.0

    @pl.when(me == 0)
    def _():
        spread(0, g_ref, store_u)

    @pl.when(me > 0)
    def _():
        for distance in range(RING):
            chunk = (me - distance + 1 + RING) % RING
            u_ref[chunk, GUARD : GUARD + tall, :] = blocks[distance][...]

    for t in range(tiles):
        points_ref[:, t * LANES : (t + 1) * LANES] = u_ref[t, inner : inner + rows, :]
    for step in range(STEPS - 1):
        src, dst = (u_ref, w_ref) if step % 2 == 0 else (w_ref, u_ref)

        def body(row, src=src, dst=dst):
            out, _ = stepped(src, (), row, rows_of(c_ref, (0, 1, 2), tiles + 1, row))
            for t in range(tiles):
                dst[t, pl.ds(row, 8), :] = out[t]

        each_block(GUARD, GUARD + tall, body)
    for t in range(tiles):
        last_ref[:, t * LANES : (t + 1) * LANES] = w_ref[t, inner : inner + rows, :]


def call(kernel, outs, scratch, cost, *args):
    flops, moved = cost
    vmem = pl.BlockSpec(memory_space=pltpu.VMEM)
    return pl.pallas_call(
        kernel,
        out_shape=[jax.ShapeDtypeStruct(s, jnp.float32) for s in outs],
        in_specs=[vmem] * len(args),
        out_specs=[vmem] * len(outs),
        scratch_shapes=[pltpu.VMEM(s, jnp.float32) for s in scratch],
        cost_estimate=pl.CostEstimate(flops=flops, bytes_accessed=moved, transcendentals=0),
        compiler_params=pltpu.CompilerParams(vmem_limit_bytes=56 << 20),
    )(*args)


def local(guess, kappa, rate):
    intervals, strips = lax.axis_size("tm"), lax.axis_size("space")
    state = guess[0]
    rows, columns = state.shape
    tiles = columns // LANES
    edges = jnp.stack([state, kappa, rate])
    up = [(i, i + 1) for i in range(strips - 1)]
    down = [(i + 1, i) for i in range(strips - 1)]
    lo = lax.ppermute(edges[:, rows - HALO :], "space", up)
    hi = lax.ppermute(edges[:, :HALO], "space", down)

    frame = rows + 2 * FRAME
    ext = rows + 2 * HALO + 2 * GUARD
    wide = frame + 2 * GUARD
    packed, own = call(
        relax_kernel,
        [(RING, frame + PACK, LANES), (3, 2, wide, LANES)],
        [(tiles + 1, ext, LANES), (tiles + 1, ext, LANES), (3, tiles + 1, ext, LANES)],
        (40 * rows * columns, 16 * rows * columns),
        state, kappa, rate, lo, hi,
    )
    rings = [[(RING * m + i - 1) % intervals for i in range(RING)] for m in range(intervals // RING)]
    fields = lax.all_to_all(packed, "tm", 0, 0, axis_index_groups=rings, tiled=True)
    four = (GROUP, 2, wide, LANES)
    later_d, sent = call(
        later_kernel, [four, (frame + PACK, LANES)], [four, four],
        (20 * rows * columns, 8 * rows * columns), fields, own,
    )
    got = lax.ppermute(sent, "tm", [(i, i + RING) for i in range(intervals - RING)]
                       + [(intervals - RING + i, i) for i in range(RING)])
    tall = rows + 2 * TAIL
    d, one, half = call(
        earlier_kernel, [four, (1, 2, wide, LANES), (RING, tall, LANES)], [four, four],
        (20 * rows * columns, 8 * rows * columns), fields, own, later_d,
    )
    (out,) = call(
        last_kernel, [(RING, tall, LANES)], [(1, 2, wide, LANES)] * 2,
        (4 * rows * columns, 4 * rows * columns), got, own, d, one, half,
    )
    blocks = []
    for distance in range(RING):
        pairs = []
        for m in range(intervals // RING):
            for i in range(RING):
                source = (RING * m + i - 1) % intervals
                field = (source + distance - 1) % RING
                pairs.append((source, (RING * m + 1 + field) % intervals))
        blocks.append(lax.ppermute(out[distance], "tm", pairs))
    c_points, last_fine = call(
        fine_kernel, [(rows, columns)] * 2,
        [(tiles + 1, tall + 2 * GUARD, LANES)] * 2 + [(3, tiles + 1, tall + 2 * GUARD, LANES)],
        (30 * rows * columns, 16 * rows * columns),
        state, kappa, rate, lo, hi, *blocks,
    )
    return c_points[None], last_fine[None]


def solution(mesh):
    return jax.shard_map(
        local,
        mesh=mesh,
        in_specs=(P("tm", "space", None), P("space", None), P("space", None)),
        out_specs=(P("tm", "space", None), P("tm", "space", None)),
        check_vma=False,
    )
```

```python
import functools

import jax
import jax.numpy as jnp
from jax import lax
from jax.experimental import pallas as pl
from jax.experimental.pallas import tpu as pltpu
from jax.sharding import PartitionSpec as P

STEPS = 4
GROUP = 4
DIFFUSION = 0.05
RING = 8
HALO = 24
LANES = 128
FRAME = 16
EDGE = 11
PACK = 64
TAIL = 4
GUARD = 8
RELAX = (96,16)
SUB = 8
MARCH, CHAIN, FINE = 96, 288, 88


def lane_index(height=8):
    return lax.broadcasted_iota(jnp.int32, (height, LANES), 1)


def neighbour_sum(tiles, up, down):
    lane = lane_index(tiles[0].shape[0])
    count = len(tiles)
    right_turned = [pltpu.roll(t, 1, 1) for t in tiles]
    left_turned = [pltpu.roll(t, LANES - 1, 1) for t in tiles]
    sums = []
    for i in range(count):
        left = jnp.where(lane == 0, right_turned[i - 1], right_turned[i])
        right = jnp.where(lane == LANES - 1, left_turned[(i + 1) % count], left_turned[i])
        sums.append((up[i] + down[i]) + (left + right))
    return sums


def stepped(ref, at, row, coefs):
    count, height = len(coefs), coefs[0][0].shape[0]
    tiles = [ref[at + (i, pl.ds(row, height), slice(None))] for i in range(count)]
    up = [ref[at + (i, pl.ds(row - 1, height), slice(None))] for i in range(count)]
    down = [ref[at + (i, pl.ds(row + 1, height), slice(None))] for i in range(count)]
    sums = neighbour_sum(tiles, up, down)
    out = [k * s + c * (m - r * (c * c)) for c, s, (k, r, m) in zip(tiles, sums, coefs)]
    return out, tiles


def rows_of(ref, kinds, count, row, height):
    return [tuple(ref[k, i, pl.ds(row, height), :] for k in kinds) for i in range(count)]


def each_block(first, last, body, height):
    assert (last - first) % height == 0

    def trip(i, carry):
        row = pl.multiple_of(first + height * i, 8)
        for part in range(0, height, SUB):
            body(row + part)
        return carry

    lax.fori_loop(0, (last - first) // height, trip, 0)


def relax_kernel(g_ref, k_ref, r_ref, lo_ref, hi_ref, packed_ref, own_ref, u_ref, w_ref, c_ref):
    rows, columns = g_ref.shape
    tiles = columns // LANES
    ext = rows + 2 * HALO
    top = GUARD + HALO
    zero8 = jnp.zeros((GUARD, LANES), jnp.float32)

    def fill(put, body_ref, part):
        for t in range(tiles):
            cols = slice(t * LANES, (t + 1) * LANES)
            put(t, GUARD, HALO, lambda a, n: lo_ref[part, pl.ds(a, n), cols])
            put(t, top, rows, lambda a, n: body_ref[pl.ds(a, n), cols])
            put(t, top + rows, HALO, lambda a, n: hi_ref[part, pl.ds(a, n), cols])

    def put_u(t, at, n, load):
        u_ref[t, at : at + n, :] = load(0, n)

    def put_k(t, at, n, load):
        c_ref[0, t, at : at + n, :] = DIFFUSION * load(0, n)

    def put_r(t, at, n, load):
        rate = load(0, n)
        c_ref[1, t, at : at + n, :] = rate
        c_ref[2, t, at : at + n, :] = 1.0 - 4.0 * c_ref[0, t, at : at + n, :] + rate

    fill(put_u, g_ref, 0)
    fill(put_k, k_ref, 1)
    fill(put_r, r_ref, 2)
    pad = jnp.zeros((ext + 2 * GUARD, LANES), jnp.float32)
    u_ref[tiles] = pad
    w_ref[tiles] = pad
    for kind in range(2):
        c_ref[kind, tiles] = pad
    c_ref[2, tiles] = pad + 1.0
    for t in range(tiles):
        for ref in (u_ref, w_ref):
            ref[t, 0:GUARD, :] = zero8
            ref[t, GUARD + ext : ext + 2 * GUARD, :] = zero8

    def march(src, dst, first, last):
        height = next(h for h in RELAX if (last - first) % h == 0)

        def body(row):
            out, _ = stepped(src, (), row, rows_of(c_ref, (0, 1, 2), tiles + 1, row, SUB))
            for t in range(tiles):
                dst[t, pl.ds(row, SUB), :] = out[t]

        each_block(first, last, body, height)

    march(u_ref, w_ref, GUARD, GUARD + ext - 16)
    march(u_ref, w_ref, GUARD + ext - 16, GUARD + ext)
    march(w_ref, u_ref, GUARD + 8, GUARD + ext - 8)
    march(u_ref, w_ref, GUARD + 8, GUARD + ext - 8)
    march(w_ref, u_ref, GUARD + 8, GUARD + ext - 8)

    frame = rows + 2 * FRAME
    base = top - FRAME
    lane = lane_index()
    for c in range(RING):
        packed_ref[c, 0:frame, :] = u_ref[c, base : base + frame, :]
        after, before = c + 1, (c - 1) % (tiles + 1)
        for block in range(PACK // 8):
            acc = jnp.zeros((8, LANES), jnp.float32)
            for part in range(pl.cdiv(frame, PACK)):
                at = part * PACK + block * 8
                if at < frame:
                    edge = jnp.where(
                        lane < LANES // 2,
                        u_ref[after, base + at : base + at + 8, :],
                        u_ref[before, base + at : base + at + 8, :],
                    )
                    begin = 2 * EDGE * part
                    turned = pltpu.roll(edge, EDGE + begin, 1)
                    acc = jnp.where((lane >= begin) & (lane < begin + 2 * EDGE), turned, acc)
            packed_ref[c, frame + 8 * block : frame + 8 * block + 8, :] = acc

    mine = (lax.axis_index("tm") + 1) % RING
    after, before = mine + 1, lax.rem(mine + tiles, tiles + 1)
    near = (lane < EDGE) | (lane >= LANES - EDGE)
    for kind in range(3):
        own_ref[kind, 0, 0:GUARD, :] = zero8
        own_ref[kind, 1, 0:GUARD, :] = zero8
        own_ref[kind, 0, GUARD + frame :, :] = zero8
        own_ref[kind, 1, GUARD + frame :, :] = zero8

        def body(row, kind=kind):
            src = row + base - GUARD
            own_ref[kind, 0, pl.ds(row, 8), :] = c_ref[kind, mine, pl.ds(src, 8), :]
            edge = jnp.where(
                lane < LANES // 2,
                c_ref[kind, after, pl.ds(src, 8), :],
                c_ref[kind, before, pl.ds(src, 8), :],
            )
            far = 1.0 if kind == 2 else 0.0
            edge = jnp.where(near, edge, far)
            own_ref[kind, 1, pl.ds(row, 8), :] = edge
            less = STEPS - 1.0 if kind == 2 else 0.0
            own_ref[kind + 3, 0, pl.ds(row, 8), :] = STEPS * c_ref[kind, mine, pl.ds(src, 8), :] - less
            own_ref[kind + 3, 1, pl.ds(row, 8), :] = STEPS * edge - less

        each_block(GUARD, GUARD + frame, body, 8)


def unpack(src_ref, at, dst_ref, to, frame):
    zero8 = jnp.zeros((GUARD, LANES), jnp.float32)
    for i in range(2):
        dst_ref[to, i, 0:GUARD, :] = zero8
        dst_ref[to, i, GUARD + frame : frame + 2 * GUARD, :] = zero8
    dst_ref[to, 0, GUARD : GUARD + frame, :] = src_ref[at + (slice(0, frame),)]
    for part in range(pl.cdiv(frame, PACK)):
        count = min(PACK, frame - part * PACK)
        block = src_ref[at + (slice(frame, frame + count),)]
        turned = pltpu.roll(block, (-(2 * EDGE * part + EDGE)) % LANES, 1)
        dst_ref[to, 1, GUARD + part * PACK : GUARD + part * PACK + count, :] = turned


def pack(src_ref, at, dst_ref, frame):
    lane = lane_index()
    dst_ref[0:frame, :] = src_ref[at, 0, GUARD : GUARD + frame, :]
    for block in range(PACK // 8):
        acc = jnp.zeros((8, LANES), jnp.float32)
        for part in range(pl.cdiv(frame, PACK)):
            row = part * PACK + block * 8
            if row < frame:
                begin = 2 * EDGE * part
                edge = src_ref[at, 1, GUARD + row : GUARD + row + 8, :]
                turned = pltpu.roll(edge, EDGE + begin, 1)
                acc = jnp.where((lane >= begin) & (lane < begin + 2 * EDGE), turned, acc)
        dst_ref[frame + 8 * block : frame + 8 * block + 8, :] = acc


def coarse_coefs(own_ref, row):
    return rows_of(own_ref, (3, 4, 5), 2, row, SUB)


def defects(in_ref, first, own_ref, x_ref, y_ref, d_ref, frame):
    for f in range(GROUP):
        unpack(in_ref, (first + f,), x_ref, f, frame)
        zero8 = jnp.zeros((GUARD, LANES), jnp.float32)
        for i in range(2):
            y_ref[f, i, 0:GUARD, :] = zero8
            y_ref[f, i, GUARD + frame : frame + 2 * GUARD, :] = zero8
    for step in range(STEPS):
        src, dst = (x_ref, y_ref) if step % 2 == 0 else (y_ref, x_ref)

        def body(row, step=step, src=src, dst=dst):
            coefs = rows_of(own_ref, (0, 1, 2), 2, row, SUB)
            for f in range(GROUP):
                out, old = stepped(src, (f,), row, coefs)
                for i in range(2):
                    dst[f, i, pl.ds(row, SUB), :] = out[i]
                    if step == 0:
                        d_ref[f, i, pl.ds(row, SUB), :] = STEPS * out[i] - (STEPS - 1.0) * old[i]
                    if step == STEPS - 1:
                        d_ref[f, i, pl.ds(row, SUB), :] = out[i] - d_ref[f, i, pl.ds(row, SUB), :]

        each_block(GUARD, GUARD + frame, body, MARCH)


def chain_step(src_ref, at, dst_ref, to, own_ref, d_ref, which, frame, also=None):
    def body(row):
        out, _ = stepped(src_ref, (at,), row, coarse_coefs(own_ref, row))
        for i in range(2):
            value = out[i] + d_ref[which, i, pl.ds(row, SUB), :]
            dst_ref[to, i, pl.ds(row, SUB), :] = value

    each_block(GUARD, GUARD + frame, body, CHAIN)


def later_kernel(in_ref, own_ref, d_ref, sent_ref, x_ref, y_ref):
    frame = in_ref.shape[1] - PACK
    defects(in_ref, GROUP, own_ref, x_ref, y_ref, d_ref, frame)
    chain_step(x_ref, 0, y_ref, 0, own_ref, d_ref, 1, frame)
    chain_step(y_ref, 0, x_ref, 0, own_ref, d_ref, 2, frame)
    chain_step(x_ref, 0, y_ref, 0, own_ref, d_ref, 3, frame)
    pack(y_ref, 0, sent_ref, frame)


def emit(src_ref, at, out_ref, field, strip):
    z = lax.axis_index("tm") % RING
    slot = (field + 1 - z + RING) % RING
    begin = GUARD + FRAME - TAIL
    out_ref[slot] = src_ref[at, 0, begin : begin + strip + 2 * TAIL, :]


def earlier_kernel(in_ref, own_ref, later_d_ref, d_ref, one_ref, out_ref, x_ref, y_ref):
    frame = in_ref.shape[1] - PACK
    strip = frame - 2 * FRAME
    defects(in_ref, 0, own_ref, x_ref, y_ref, d_ref, frame)
    unpack(in_ref, (1,), one_ref, 0, frame)

    @pl.when(lax.axis_index("tm") + 1 < RING)
    def _():
        x_ref[0] = one_ref[0]

    @pl.when(lax.axis_index("tm") == lax.axis_size("tm") - 1)
    def _():
        x_ref[0] = one_ref[0]

    chain_step(x_ref, 0, y_ref, 0, own_ref, d_ref, 1, frame)
    chain_step(y_ref, 0, x_ref, 0, own_ref, d_ref, 2, frame)
    chain_step(x_ref, 0, y_ref, 0, own_ref, d_ref, 3, frame)
    for i in range(GROUP):
        src, dst = (y_ref, x_ref) if i % 2 == 0 else (x_ref, y_ref)
        chain_step(src, 0, dst, 0, own_ref, later_d_ref, i, frame)
        emit(dst, 0, out_ref, GROUP + i, strip)


def last_kernel(got_ref, own_ref, d_ref, one_ref, half_ref, out_ref, x_ref, y_ref):
    frame = got_ref.shape[0] - PACK
    strip = frame - 2 * FRAME
    out_ref[...] = half_ref[...]
    unpack(got_ref, (), x_ref, 0, frame)
    zero8 = jnp.zeros((GUARD, LANES), jnp.float32)
    for i in range(2):
        y_ref[0, i, 0:GUARD, :] = zero8
        y_ref[0, i, GUARD + frame : frame + 2 * GUARD, :] = zero8
    for i in range(GROUP):
        src, dst = (x_ref, y_ref) if i % 2 == 0 else (y_ref, x_ref)
        chain_step(src, 0, dst, 0, own_ref, d_ref, i, frame)
        if i == 0:
            member = (lax.axis_index("tm") + 1) % lax.axis_size("tm")

            @pl.when(member < RING)
            def _():
                dst[0] = one_ref[0]

        emit(dst, 0, out_ref, i, strip)


def fine_kernel(g_ref, k_ref, r_ref, lo_ref, hi_ref, *refs):
    blocks, (points_ref, last_ref, u_ref, w_ref, c_ref) = refs[:RING], refs[RING:]
    rows, columns = g_ref.shape
    tiles = columns // LANES
    tall = rows + 2 * TAIL
    zero8 = jnp.zeros((GUARD, LANES), jnp.float32)
    me = lax.axis_index("tm")
    for ref in (u_ref, w_ref):
        ref[tiles] = jnp.zeros((tall + 2 * GUARD, LANES), jnp.float32)
        for t in range(tiles):
            ref[t, 0:GUARD, :] = zero8
            ref[t, GUARD + tall : tall + 2 * GUARD, :] = zero8
    inner = GUARD + TAIL

    def spread(part, body_ref, store):
        for t in range(tiles):
            cols = slice(t * LANES, (t + 1) * LANES)
            store(t, GUARD, TAIL, lo_ref[part, HALO - TAIL : HALO, cols])
            store(t, inner, rows, body_ref[:, cols])
            store(t, inner + rows, TAIL, hi_ref[part, 0:TAIL, cols])

    def store_k(t, at, n, value):
        c_ref[0, t, at : at + n, :] = DIFFUSION * value

    def store_r(t, at, n, value):
        c_ref[1, t, at : at + n, :] = value
        c_ref[2, t, at : at + n, :] = 1.0 - 4.0 * c_ref[0, t, at : at + n, :] + value

    def store_u(t, at, n, value):
        u_ref[t, at : at + n, :] = value

    spread(1, k_ref, store_k)
    spread(2, r_ref, store_r)
    pad = jnp.zeros((tall + 2 * GUARD, LANES), jnp.float32)
    c_ref[0, tiles] = pad
    c_ref[1, tiles] = pad
    c_ref[2, tiles] = pad + 1.0

    @pl.when(me == 0)
    def _():
        spread(0, g_ref, store_u)

    @pl.when(me > 0)
    def _():
        for distance in range(RING):
            chunk = (me - distance + 1 + RING) % RING
            u_ref[chunk, GUARD : GUARD + tall, :] = blocks[distance][...]

    for t in range(tiles):
        points_ref[:, t * LANES : (t + 1) * LANES] = u_ref[t, inner : inner + rows, :]
    for step in range(STEPS - 1):
        src, dst = (u_ref, w_ref) if step % 2 == 0 else (w_ref, u_ref)

        def body(row, src=src, dst=dst):
            out, _ = stepped(src, (), row, rows_of(c_ref, (0, 1, 2), tiles + 1, row, SUB))
            for t in range(tiles):
                dst[t, pl.ds(row, SUB), :] = out[t]

        each_block(GUARD, GUARD + tall, body, FINE)
    for t in range(tiles):
        last_ref[:, t * LANES : (t + 1) * LANES] = w_ref[t, inner : inner + rows, :]


def call(kernel, outs, scratch, cost, *args):
    flops, moved = cost
    vmem = pl.BlockSpec(memory_space=pltpu.VMEM)
    return pl.pallas_call(
        kernel,
        out_shape=[jax.ShapeDtypeStruct(s, jnp.float32) for s in outs],
        in_specs=[vmem] * len(args),
        out_specs=[vmem] * len(outs),
        scratch_shapes=[pltpu.VMEM(s, jnp.float32) for s in scratch],
        cost_estimate=pl.CostEstimate(flops=flops, bytes_accessed=moved, transcendentals=0),
        compiler_params=pltpu.CompilerParams(vmem_limit_bytes=24 << 20),
    )(*args)


def local(guess, kappa, rate):
    intervals, strips = lax.axis_size("tm"), lax.axis_size("space")
    state = guess[0]
    rows, columns = state.shape
    tiles = columns // LANES
    edges = jnp.stack([state, kappa, rate])
    up = [(i, i + 1) for i in range(strips - 1)]
    down = [(i + 1, i) for i in range(strips - 1)]
    lo = lax.ppermute(edges[:, rows - HALO :], "space", up)
    hi = lax.ppermute(edges[:, :HALO], "space", down)

    frame = rows + 2 * FRAME
    ext = rows + 2 * HALO + 2 * GUARD
    wide = frame + 2 * GUARD
    packed, own = call(
        relax_kernel,
        [(RING, frame + PACK, LANES), (6, 2, wide, LANES)],
        [(tiles + 1, ext, LANES), (tiles + 1, ext, LANES), (3, tiles + 1, ext, LANES)],
        (40 * rows * columns, 16 * rows * columns),
        state, kappa, rate, lo, hi,
    )
    rings = [[(RING * m + i - 1) % intervals for i in range(RING)] for m in range(intervals // RING)]
    fields = lax.all_to_all(packed, "tm", 0, 0, axis_index_groups=rings, tiled=True)
    four = (GROUP, 2, wide, LANES)
    later_d, sent = call(
        later_kernel, [four, (frame + PACK, LANES)], [four, four],
        (20 * rows * columns, 8 * rows * columns), fields, own,
    )
    got = lax.ppermute(sent, "tm", [(i, i + RING) for i in range(intervals - RING)]
                       + [(intervals - RING + i, i) for i in range(RING)])
    tall = rows + 2 * TAIL
    d, one, half = call(
        earlier_kernel, [four, (1, 2, wide, LANES), (RING, tall, LANES)], [four, four],
        (20 * rows * columns, 8 * rows * columns), fields, own, later_d,
    )
    (out,) = call(
        last_kernel, [(RING, tall, LANES)], [(1, 2, wide, LANES)] * 2,
        (4 * rows * columns, 4 * rows * columns), got, own, d, one, half,
    )
    blocks = []
    for distance in range(RING):
        pairs = []
        for m in range(intervals // RING):
            for i in range(RING):
                source = (RING * m + i - 1) % intervals
                field = (source + distance - 1) % RING
                pairs.append((source, (RING * m + 1 + field) % intervals))
        blocks.append(lax.ppermute(out[distance], "tm", pairs))
    c_points, last_fine = call(
        fine_kernel, [(rows, columns)] * 2,
        [(tiles + 1, tall + 2 * GUARD, LANES)] * 2 + [(3, tiles + 1, tall + 2 * GUARD, LANES)],
        (30 * rows * columns, 16 * rows * columns),
        state, kappa, rate, lo, hi, *blocks,
    )
    return c_points[None], last_fine[None]


def solution(mesh):
    return jax.shard_map(
        local,
        mesh=mesh,
        in_specs=(P("tm", "space", None), P("space", None), P("space", None)),
        out_specs=(P("tm", "space", None), P("tm", "space", None)),
        check_vma=False,
    )
```

```python
import functools

import jax
import jax.numpy as jnp
from jax import lax
from jax.experimental import pallas as pl
from jax.experimental.pallas import tpu as pltpu
from jax.sharding import PartitionSpec as P

STEPS = 4
GROUP = 4
DIFFUSION = 0.05
RING = 8
HALO = 24
LANES = 128
FRAME = 16
EDGE = 11
SKIP, NEAR = 8, 4
TAIL = 4
GUARD = 8
SENDS = (3, 5, 4, 2, 6, 1, 7)
ORDER = (0, 1, 7, 2, 6, 4, 5, 3)
RELAX = (96,16)
SUB = 8
MARCH, CHAIN, FINE = 288, 288, 88
DEFECT_FLOPS = 20_000_000


def lane_index(height=8):
    return lax.broadcasted_iota(jnp.int32, (height, LANES), 1)


def neighbour_sum(tiles, up, down):
    lane = lane_index(tiles[0].shape[0])
    count = len(tiles)
    right_turned = [pltpu.roll(t, 1, 1) for t in tiles]
    left_turned = [pltpu.roll(t, LANES - 1, 1) for t in tiles]
    sums = []
    for i in range(count):
        left = jnp.where(lane == 0, right_turned[i - 1], right_turned[i])
        right = jnp.where(lane == LANES - 1, left_turned[(i + 1) % count], left_turned[i])
        sums.append((up[i] + down[i]) + (left + right))
    return sums


def stepped(ref, at, row, coefs):
    count, height = len(coefs), coefs[0][0].shape[0]
    tiles = [ref[at + (i, pl.ds(row, height), slice(None))] for i in range(count)]
    up = [ref[at + (i, pl.ds(row - 1, height), slice(None))] for i in range(count)]
    down = [ref[at + (i, pl.ds(row + 1, height), slice(None))] for i in range(count)]
    sums = neighbour_sum(tiles, up, down)
    out = [k * s + c * (m - r * (c * c)) for c, s, (k, r, m) in zip(tiles, sums, coefs)]
    return out, tiles


def rows_of(ref, kinds, count, row, height):
    return [tuple(ref[k, i, pl.ds(row, height), :] for k in kinds) for i in range(count)]


def each_block(first, last, body, height):
    assert (last - first) % height == 0

    def trip(i, carry):
        row = pl.multiple_of(first + height * i, 8)
        for part in range(0, height, SUB):
            body(row + part)
        return carry

    lax.fori_loop(0, (last - first) // height, trip, 0)


def relax_kernel(g_ref, k_ref, r_ref, lo_ref, hi_ref, packed_ref, own_ref, u_ref, w_ref, c_ref):
    rows, columns = g_ref.shape
    tiles = columns // LANES
    ext = rows + 2 * HALO
    top = GUARD + HALO
    zero8 = jnp.zeros((GUARD, LANES), jnp.float32)

    def fill(put, body_ref, part):
        for t in range(tiles):
            cols = slice(t * LANES, (t + 1) * LANES)
            put(t, GUARD, HALO, lambda a, n: lo_ref[part, pl.ds(a, n), cols])
            put(t, top, rows, lambda a, n: body_ref[pl.ds(a, n), cols])
            put(t, top + rows, HALO, lambda a, n: hi_ref[part, pl.ds(a, n), cols])

    def put_u(t, at, n, load):
        u_ref[t, at : at + n, :] = load(0, n)

    def put_k(t, at, n, load):
        c_ref[0, t, at : at + n, :] = DIFFUSION * load(0, n)

    def put_r(t, at, n, load):
        rate = load(0, n)
        c_ref[1, t, at : at + n, :] = rate
        c_ref[2, t, at : at + n, :] = 1.0 - 4.0 * c_ref[0, t, at : at + n, :] + rate

    fill(put_u, g_ref, 0)
    fill(put_k, k_ref, 1)
    fill(put_r, r_ref, 2)
    pad = jnp.zeros((ext + 2 * GUARD, LANES), jnp.float32)
    u_ref[tiles] = pad
    w_ref[tiles] = pad
    for kind in range(2):
        c_ref[kind, tiles] = pad
    c_ref[2, tiles] = pad + 1.0
    for t in range(tiles):
        for ref in (u_ref, w_ref):
            ref[t, 0:GUARD, :] = zero8
            ref[t, GUARD + ext : ext + 2 * GUARD, :] = zero8

    def march(src, dst, first, last):
        height = next(h for h in RELAX if (last - first) % h == 0)

        def body(row):
            out, _ = stepped(src, (), row, rows_of(c_ref, (0, 1, 2), tiles + 1, row, SUB))
            for t in range(tiles):
                dst[t, pl.ds(row, SUB), :] = out[t]

        each_block(first, last, body, height)

    march(u_ref, w_ref, GUARD, GUARD + ext - 16)
    march(u_ref, w_ref, GUARD + ext - 16, GUARD + ext)
    march(w_ref, u_ref, GUARD + 8, GUARD + ext - 8)
    march(u_ref, w_ref, GUARD + 8, GUARD + ext - 8)
    march(w_ref, u_ref, GUARD + 8, GUARD + ext - 8)

    frame = rows + 2 * FRAME
    base = top - FRAME
    lane = lane_index()
    member = (lax.axis_index("tm") + 1) % RING
    for distance in range(RING):
        c = (member + distance) % RING
        after, before = c + 1, lax.rem(c + tiles, tiles + 1)
        packed_ref[distance, 0:frame, :] = u_ref[c, base : base + frame, :]

        def edge(block, after=after, before=before):
            at = base + 8 * block
            return jnp.where(lane < LANES // 2, u_ref[after, at : at + 8, :], u_ref[before, at : at + 8, :])

        pack_edges(edge, frame // 8, EDGE, packed_ref, (distance,), frame)

    mine = member
    after, before = mine + 1, lax.rem(mine + tiles, tiles + 1)
    near = (lane < EDGE) | (lane >= LANES - EDGE)
    for kind in range(3):
        own_ref[kind, 0, 0:GUARD, :] = zero8
        own_ref[kind, 1, 0:GUARD, :] = zero8
        own_ref[kind, 0, GUARD + frame :, :] = zero8
        own_ref[kind, 1, GUARD + frame :, :] = zero8

        def body(row, kind=kind):
            src = row + base - GUARD
            own_ref[kind, 0, pl.ds(row, 8), :] = c_ref[kind, mine, pl.ds(src, 8), :]
            edge = jnp.where(
                lane < LANES // 2,
                c_ref[kind, after, pl.ds(src, 8), :],
                c_ref[kind, before, pl.ds(src, 8), :],
            )
            far = 1.0 if kind == 2 else 0.0
            edge = jnp.where(near, edge, far)
            own_ref[kind, 1, pl.ds(row, 8), :] = edge
            less = STEPS - 1.0 if kind == 2 else 0.0
            own_ref[kind + 3, 0, pl.ds(row, 8), :] = STEPS * c_ref[kind, mine, pl.ds(src, 8), :] - less
            own_ref[kind + 3, 1, pl.ds(row, 8), :] = STEPS * edge - less

        each_block(GUARD, GUARD + frame, body, 8)


def parts_of(blocks, edge):
    return pl.cdiv(blocks, LANES // (2 * edge))


def pack_edges(load, blocks, edge, dst_ref, at, row):
    lane = lane_index()
    per = parts_of(blocks, edge)
    for j in range(per):
        acc = jnp.zeros((8, LANES), jnp.float32)
        for part in range(pl.cdiv(blocks, per)):
            if part * per + j < blocks:
                begin = 2 * edge * part
                turned = pltpu.roll(load(part * per + j), edge + begin, 1)
                acc = jnp.where((lane >= begin) & (lane < begin + 2 * edge), turned, acc)
        dst_ref[at + (slice(row + 8 * j, row + 8 * j + 8), slice(None))] = acc


def unpack(src_ref, dst_ref, skip, height, edge):
    tall = dst_ref.shape[1]
    begin = GUARD + skip
    for i in range(2):
        dst_ref[i, 0:begin, :] = jnp.zeros((begin, LANES), jnp.float32)
        dst_ref[i, begin + height :, :] = jnp.zeros((tall - begin - height, LANES), jnp.float32)
    dst_ref[0, begin : begin + height, :] = src_ref[0:height, :]
    blocks = height // 8
    per = parts_of(blocks, edge)
    for part in range(pl.cdiv(blocks, per)):
        count = 8 * min(per, blocks - part * per)
        turned = pltpu.roll(src_ref[height : height + count, :], (-(2 * part + 1) * edge) % LANES, 1)
        dst_ref[1, begin + 8 * per * part : begin + 8 * per * part + count, :] = turned


def guard(ref):
    tall = ref.shape[1]
    for i in range(2):
        ref[i, 0:GUARD, :] = jnp.zeros((GUARD, LANES), jnp.float32)
        ref[i, tall - GUARD :, :] = jnp.zeros((GUARD, LANES), jnp.float32)


def ring_member():
    member = (lax.axis_index("tm") + 1) % lax.axis_size("tm")
    return member % RING, member < RING


def coarse_coefs(own_ref, row):
    return rows_of(own_ref, (3, 4, 5), 2, row, SUB)


def defect_kernel(distance, in_ref, own_ref, d_ref, p_ref, x_ref, y_ref):
    frame = x_ref.shape[1] - 2 * GUARD
    unpack(in_ref, x_ref, 0, frame, EDGE)
    guard(y_ref)
    guard(p_ref)
    for step in range(STEPS):
        src, dst = (x_ref, y_ref) if step % 2 == 0 else (y_ref, x_ref)
        dst = p_ref if step == STEPS - 1 else dst

        def body(row, step=step, src=src, dst=dst):
            out, old = stepped(src, (), row, rows_of(own_ref, (0, 1, 2), 2, row, SUB))
            for i in range(2):
                dst[i, pl.ds(row, SUB), :] = out[i]
                if step == 0:
                    d_ref[i, pl.ds(row, SUB), :] = STEPS * out[i] - (STEPS - 1.0) * old[i]
                if step == STEPS - 1:
                    d_ref[i, pl.ds(row, SUB), :] = out[i] - d_ref[i, pl.ds(row, SUB), :]

        each_block(GUARD, GUARD + frame, body, MARCH)
    member, first = ring_member()

    @pl.when(first & ((member - distance + RING) % RING == 1))
    def _():
        unpack(in_ref, p_ref, 0, frame, EDGE)


def chain_step(src_ref, dst_ref, own_ref, d_ref, which, frame):
    def body(row):
        out, _ = stepped(src_ref, (), row, coarse_coefs(own_ref, row))
        for i in range(2):
            dst_ref[i, pl.ds(row, SUB), :] = out[i] + d_ref[which, i, pl.ds(row, SUB), :]

    each_block(GUARD, GUARD + frame, body, CHAIN)


def later_kernel(own_ref, *refs):
    (d_refs, p_refs), (all_ref, one_ref, sent_ref, x_ref, y_ref) = (refs[:RING], refs[RING : 2 * RING]), refs[2 * RING :]
    frame = x_ref.shape[1] - 2 * GUARD
    member, first = ring_member()
    begin = jnp.where(first, 1, 0)
    for at, distance in enumerate((0,) + SENDS):
        field = (member - distance + RING) % RING
        all_ref[field] = d_refs[at][...]

        @pl.when(field == GROUP)
        def _(at=at):
            x_ref[...] = p_refs[at][...]

        @pl.when(field == begin)
        def _(at=at):
            one_ref[...] = p_refs[at][...]

    guard(y_ref)
    chain_step(x_ref, y_ref, own_ref, all_ref, GROUP + 1, frame)
    chain_step(y_ref, x_ref, own_ref, all_ref, GROUP + 2, frame)
    chain_step(x_ref, y_ref, own_ref, all_ref, GROUP + 3, frame)
    at = GUARD + SKIP
    height = frame - 2 * SKIP
    sent_ref[0:height, :] = y_ref[0, at : at + height, :]
    pack_edges(lambda b: y_ref[1, at + 8 * b : at + 8 * b + 8, :], height // 8, NEAR, sent_ref, (), height)


def emit(src_ref, out_ref, field, strip):
    z = lax.axis_index("tm") % RING
    slot = (field + 1 - z + RING) % RING
    begin = GUARD + FRAME - TAIL
    out_ref[slot] = src_ref[0, begin : begin + strip + 2 * TAIL, :]


def earlier_kernel(own_ref, d_ref, one_ref, out_ref, x_ref, y_ref):
    frame = x_ref.shape[1] - 2 * GUARD
    strip = frame - 2 * FRAME
    guard(x_ref)
    guard(y_ref)
    chain_step(one_ref, y_ref, own_ref, d_ref, 1, frame)
    chain_step(y_ref, x_ref, own_ref, d_ref, 2, frame)
    chain_step(x_ref, y_ref, own_ref, d_ref, 3, frame)
    for i in range(GROUP):
        src, dst = (y_ref, x_ref) if i % 2 == 0 else (x_ref, y_ref)
        chain_step(src, dst, own_ref, d_ref, GROUP + i, frame)
        emit(dst, out_ref, GROUP + i, strip)


def last_kernel(got_ref, own_ref, d_ref, one_ref, half_ref, out_ref, x_ref, y_ref):
    frame = x_ref.shape[1] - 2 * GUARD
    strip = frame - 2 * FRAME
    unpack(got_ref, x_ref, SKIP, frame - 2 * SKIP, NEAR)
    guard(y_ref)
    out_ref[...] = half_ref[...]
    _, first = ring_member()
    for i in range(GROUP):
        src, dst = (x_ref, y_ref) if i % 2 == 0 else (y_ref, x_ref)
        chain_step(src, dst, own_ref, d_ref, i, frame)
        if i == 0:

            @pl.when(first)
            def _():
                dst[...] = one_ref[...]

        emit(dst, out_ref, i, strip)


def fine_kernel(g_ref, k_ref, r_ref, lo_ref, hi_ref, *refs):
    blocks, (points_ref, last_ref, u_ref, w_ref, c_ref) = refs[:RING], refs[RING:]
    rows, columns = g_ref.shape
    tiles = columns // LANES
    tall = rows + 2 * TAIL
    zero8 = jnp.zeros((GUARD, LANES), jnp.float32)
    me = lax.axis_index("tm")
    for ref in (u_ref, w_ref):
        ref[tiles] = jnp.zeros((tall + 2 * GUARD, LANES), jnp.float32)
        for t in range(tiles):
            ref[t, 0:GUARD, :] = zero8
            ref[t, GUARD + tall : tall + 2 * GUARD, :] = zero8
    inner = GUARD + TAIL

    def spread(part, body_ref, store):
        for t in range(tiles):
            cols = slice(t * LANES, (t + 1) * LANES)
            store(t, GUARD, TAIL, lo_ref[part, HALO - TAIL : HALO, cols])
            store(t, inner, rows, body_ref[:, cols])
            store(t, inner + rows, TAIL, hi_ref[part, 0:TAIL, cols])

    def store_k(t, at, n, value):
        c_ref[0, t, at : at + n, :] = DIFFUSION * value

    def store_r(t, at, n, value):
        c_ref[1, t, at : at + n, :] = value
        c_ref[2, t, at : at + n, :] = 1.0 - 4.0 * c_ref[0, t, at : at + n, :] + value

    def store_u(t, at, n, value):
        u_ref[t, at : at + n, :] = value

    spread(1, k_ref, store_k)
    spread(2, r_ref, store_r)
    pad = jnp.zeros((tall + 2 * GUARD, LANES), jnp.float32)
    c_ref[0, tiles] = pad
    c_ref[1, tiles] = pad
    c_ref[2, tiles] = pad + 1.0

    @pl.when(me == 0)
    def _():
        spread(0, g_ref, store_u)

    @pl.when(me > 0)
    def _():
        for block, distance in zip(blocks, ORDER):
            chunk = (me - distance + 1 + RING) % RING
            u_ref[chunk, GUARD : GUARD + tall, :] = block[...]

    for t in range(tiles):
        points_ref[:, t * LANES : (t + 1) * LANES] = u_ref[t, inner : inner + rows, :]
    for step in range(STEPS - 1):
        src, dst = (u_ref, w_ref) if step % 2 == 0 else (w_ref, u_ref)

        def body(row, src=src, dst=dst):
            out, _ = stepped(src, (), row, rows_of(c_ref, (0, 1, 2), tiles + 1, row, SUB))
            for t in range(tiles):
                dst[t, pl.ds(row, SUB), :] = out[t]

        each_block(GUARD, GUARD + tall, body, FINE)
    for t in range(tiles):
        last_ref[:, t * LANES : (t + 1) * LANES] = w_ref[t, inner : inner + rows, :]


def call(kernel, outs, scratch, cost, *args):
    flops, moved = cost
    vmem = pl.BlockSpec(memory_space=pltpu.VMEM)
    return pl.pallas_call(
        kernel,
        out_shape=[jax.ShapeDtypeStruct(s, jnp.float32) for s in outs],
        in_specs=[vmem] * len(args),
        out_specs=[vmem] * len(outs),
        scratch_shapes=[pltpu.VMEM(s, jnp.float32) for s in scratch],
        cost_estimate=pl.CostEstimate(flops=flops, bytes_accessed=moved, transcendentals=0),
        compiler_params=pltpu.CompilerParams(vmem_limit_bytes=24 << 20),
    )(*args)


def local(guess, kappa, rate):
    intervals, strips = lax.axis_size("tm"), lax.axis_size("space")
    state = guess[0]
    rows, columns = state.shape
    tiles = columns // LANES
    edges = jnp.stack([state, kappa, rate])
    up = [(i, i + 1) for i in range(strips - 1)]
    down = [(i + 1, i) for i in range(strips - 1)]
    lo = lax.ppermute(edges[:, rows - HALO :], "space", up)
    hi = lax.ppermute(edges[:, :HALO], "space", down)

    frame = rows + 2 * FRAME
    ext = rows + 2 * HALO + 2 * GUARD
    wide = frame + 2 * GUARD
    pair = (2, wide, LANES)
    height = frame - 2 * SKIP
    packed, own = call(
        relax_kernel,
        [(RING, frame + 8 * parts_of(frame // 8, EDGE), LANES), (6, 2, wide, LANES)],
        [(tiles + 1, ext, LANES), (tiles + 1, ext, LANES), (3, tiles + 1, ext, LANES)],
        (40 * rows * columns, 16 * rows * columns),
        state, kappa, rate, lo, hi,
    )
    phis = [None] * RING
    for distance in (0,) + SENDS:
        block = packed[distance]
        if distance:
            block = lax.ppermute(block, "tm", [
                ((RING * m + i - 1) % intervals, (RING * m + (i + distance) % RING - 1) % intervals)
                for m in range(intervals // RING) for i in range(RING)
            ])
        phis[distance] = call(
            functools.partial(defect_kernel, distance), [pair, pair], [pair, pair],
            (DEFECT_FLOPS, rows * columns), block, own,
        )
    every, one, sent = call(
        later_kernel,
        [(RING,) + pair, pair, (height + 8 * parts_of(height // 8, NEAR), LANES)], [pair, pair],
        (4 * rows * columns, 4 * rows * columns), own, *(phis[at][0] for at in (0,) + SENDS), *(phis[at][1] for at in (0,) + SENDS),
    )
    got = lax.ppermute(sent, "tm", [(i, i + RING) for i in range(intervals - RING)]
                       + [(intervals - RING + i, i) for i in range(RING)])
    tall = rows + 2 * TAIL
    (half,) = call(
        earlier_kernel, [(RING, tall, LANES)], [pair, pair],
        (8 * rows * columns, 4 * rows * columns), own, every, one,
    )
    (out,) = call(
        last_kernel, [(RING, tall, LANES)], [pair, pair],
        (4 * rows * columns, 4 * rows * columns), got, own, every, one, half,
    )
    blocks = [None] * RING
    for distance in ORDER:
        pairs = []
        for m in range(intervals // RING):
            for i in range(RING):
                source = (RING * m + i - 1) % intervals
                field = (source + distance - 1) % RING
                pairs.append((source, (RING * m + 1 + field) % intervals))
        blocks[distance] = lax.ppermute(out[distance], "tm", pairs)
    c_points, last_fine = call(
        fine_kernel, [(rows, columns)] * 2,
        [(tiles + 1, tall + 2 * GUARD, LANES)] * 2 + [(3, tiles + 1, tall + 2 * GUARD, LANES)],
        (30 * rows * columns, 16 * rows * columns),
        state, kappa, rate, lo, hi, *(blocks[distance] for distance in ORDER),
    )
    return c_points[None], last_fine[None]


def solution(mesh):
    return jax.shard_map(
        local,
        mesh=mesh,
        in_specs=(P("tm", "space", None), P("space", None), P("space", None)),
        out_specs=(P("tm", "space", None), P("tm", "space", None)),
        check_vma=False,
    )
```

```python
import functools

import jax
import jax.numpy as jnp
from jax import lax
from jax.experimental import pallas as pl
from jax.experimental.pallas import tpu as pltpu
from jax.sharding import PartitionSpec as P

STEPS = 4
GROUP = 4
DIFFUSION = 0.05
RING = 8
HALO = 24
LANES = 128
FRAME = 16
EDGE = 11
SKIP, NEAR = 8, 4
TAIL = 4
GUARD = 8
SENDS = (3, 5, 4, 2, 6, 1, 7)
ORDER = (0, 1, 7, 2, 6, 4, 5, 3)
RELAX = (288,16)
SUB = 8
MARCH, CHAIN, FINE = 288, 288, 88
DEFECT_FLOPS = 20_000_000


def lane_index(height=8):
    return lax.broadcasted_iota(jnp.int32, (height, LANES), 1)


def neighbour_sum(tiles, up, down, ring):
    lane = lane_index(tiles[0].shape[0])
    count = len(tiles)
    right_turned = [pltpu.roll(t, 1, 1) for t in tiles]
    left_turned = [pltpu.roll(t, LANES - 1, 1) for t in tiles]
    sums = []
    for i in range(count):
        before = right_turned[i - 1] if ring or i > 0 else 0.0
        after = left_turned[(i + 1) % count] if ring or i + 1 < count else 0.0
        left = jnp.where(lane == 0, before, right_turned[i])
        right = jnp.where(lane == LANES - 1, after, left_turned[i])
        sums.append((up[i] + down[i]) + (left + right))
    return sums


def stepped(ref, at, row, coefs, ring=True):
    count, height = len(coefs), coefs[0][0].shape[0]
    tiles = [ref[at + (i, pl.ds(row, height), slice(None))] for i in range(count)]
    up = [ref[at + (i, pl.ds(row - 1, height), slice(None))] for i in range(count)]
    down = [ref[at + (i, pl.ds(row + 1, height), slice(None))] for i in range(count)]
    sums = neighbour_sum(tiles, up, down, ring)
    out = [k * s + c * (m - r * (c * c)) for c, s, (k, r, m) in zip(tiles, sums, coefs)]
    return out, tiles


def rows_of(ref, kinds, count, row, height):
    return [tuple(ref[k, i, pl.ds(row, height), :] for k in kinds) for i in range(count)]


def each_block(first, last, body, height):
    assert (last - first) % height == 0

    def trip(i, carry):
        row = pl.multiple_of(first + height * i, 8)
        for part in range(0, height, SUB):
            body(row + part)
        return carry

    lax.fori_loop(0, (last - first) // height, trip, 0)


def spread(put, lo_ref, body_ref, hi_ref, part, take, at):
    rows, columns = body_ref.shape
    for t in range(columns // LANES):
        cols = slice(t * LANES, (t + 1) * LANES)
        put(t, at, lo_ref[part, HALO - take : HALO, cols])
        put(t, at + take, body_ref[:, cols])
        put(t, at + take + rows, hi_ref[part, 0:take, cols])


def spread_coefs(c_ref, k_ref, r_ref, lo_ref, hi_ref, take, at):
    def put_k(t, row, value):
        c_ref[0, t, row : row + value.shape[0], :] = DIFFUSION * value

    def put_r(t, row, value):
        rows = slice(row, row + value.shape[0])
        c_ref[1, t, rows, :] = value
        c_ref[2, t, rows, :] = 1.0 - 4.0 * c_ref[0, t, rows, :] + value

    spread(put_k, lo_ref, k_ref, hi_ref, 1, take, at)
    spread(put_r, lo_ref, r_ref, hi_ref, 2, take, at)


def relax_kernel(g_ref, k_ref, r_ref, lo_ref, hi_ref, packed_ref, u_ref, w_ref, c_ref):
    rows, columns = g_ref.shape
    tiles = columns // LANES
    ext = rows + 2 * HALO
    top = GUARD + HALO
    zero8 = jnp.zeros((GUARD, LANES), jnp.float32)

    def put_u(t, row, value):
        u_ref[t, row : row + value.shape[0], :] = value

    spread(put_u, lo_ref, g_ref, hi_ref, 0, HALO, GUARD)
    spread_coefs(c_ref, k_ref, r_ref, lo_ref, hi_ref, HALO, GUARD)
    u_ref[tiles] = jnp.zeros((ext + 2 * GUARD, LANES), jnp.float32)
    for t in range(tiles):
        for ref in (u_ref, w_ref):
            ref[t, 0:GUARD, :] = zero8
            ref[t, GUARD + ext : ext + 2 * GUARD, :] = zero8

    def march(src, dst, first, last):
        height = next(h for h in RELAX if (last - first) % h == 0)

        def body(row):
            out, _ = stepped(src, (), row, rows_of(c_ref, (0, 1, 2), tiles, row, SUB), ring=False)
            for t in range(tiles):
                dst[t, pl.ds(row, SUB), :] = out[t]

        each_block(first, last, body, height)

    march(u_ref, w_ref, GUARD, GUARD + ext - 16)
    march(u_ref, w_ref, GUARD + ext - 16, GUARD + ext)
    march(w_ref, u_ref, GUARD + 8, GUARD + ext - 8)
    march(u_ref, w_ref, GUARD + 8, GUARD + ext - 8)
    march(w_ref, u_ref, GUARD + 8, GUARD + ext - 8)

    frame = rows + 2 * FRAME
    base = top - FRAME
    lane = lane_index()
    member = (lax.axis_index("tm") + 1) % RING
    for distance in range(RING):
        c = (member + distance) % RING
        after, before = c + 1, lax.rem(c + tiles, tiles + 1)
        packed_ref[distance, 0:frame, :] = u_ref[c, base : base + frame, :]

        def edge(block, after=after, before=before):
            at = base + 8 * block
            return jnp.where(lane < LANES // 2, u_ref[after, at : at + 8, :], u_ref[before, at : at + 8, :])

        pack_edges(edge, frame // 8, EDGE, packed_ref, (distance,), frame)


def coef_kernel(k_ref, r_ref, lo_ref, hi_ref, after_ref, own_ref, fine_ref, c_ref):
    del after_ref
    rows, columns = k_ref.shape
    tiles = columns // LANES
    ext = rows + 2 * HALO
    top = GUARD + HALO
    frame, tall = rows + 2 * FRAME, rows + 2 * TAIL
    base = top - FRAME
    lane = lane_index()
    zero8 = jnp.zeros((GUARD, LANES), jnp.float32)
    spread_coefs(c_ref, k_ref, r_ref, lo_ref, hi_ref, HALO, GUARD)
    pad = jnp.zeros((ext + 2 * GUARD, LANES), jnp.float32)
    for kind in range(3):
        c_ref[kind, tiles] = pad + (1.0 if kind == 2 else 0.0)
        for t in range(tiles):
            fine_ref[kind, t, 0:GUARD, :] = zero8
            fine_ref[kind, t, GUARD + tall :, :] = zero8
            fine_ref[kind, t, GUARD : GUARD + tall, :] = c_ref[kind, t, top - TAIL : top - TAIL + tall, :]
    mine = (lax.axis_index("tm") + 1) % RING
    after, before = mine + 1, lax.rem(mine + tiles, tiles + 1)
    near = (lane < EDGE) | (lane >= LANES - EDGE)
    for kind in range(3):
        own_ref[kind, 0, 0:GUARD, :] = zero8
        own_ref[kind, 1, 0:GUARD, :] = zero8
        own_ref[kind, 0, GUARD + frame :, :] = zero8
        own_ref[kind, 1, GUARD + frame :, :] = zero8

        def body(row, kind=kind):
            src = row + base - GUARD
            own_ref[kind, 0, pl.ds(row, 8), :] = c_ref[kind, mine, pl.ds(src, 8), :]
            edge = jnp.where(
                lane < LANES // 2,
                c_ref[kind, after, pl.ds(src, 8), :],
                c_ref[kind, before, pl.ds(src, 8), :],
            )
            far = 1.0 if kind == 2 else 0.0
            edge = jnp.where(near, edge, far)
            own_ref[kind, 1, pl.ds(row, 8), :] = edge
            less = STEPS - 1.0 if kind == 2 else 0.0
            own_ref[kind + 3, 0, pl.ds(row, 8), :] = STEPS * c_ref[kind, mine, pl.ds(src, 8), :] - less
            own_ref[kind + 3, 1, pl.ds(row, 8), :] = STEPS * edge - less

        each_block(GUARD, GUARD + frame, body, 8)


def parts_of(blocks, edge):
    return pl.cdiv(blocks, LANES // (2 * edge))


def pack_edges(load, blocks, edge, dst_ref, at, row):
    lane = lane_index()
    per = parts_of(blocks, edge)
    for j in range(per):
        acc = jnp.zeros((8, LANES), jnp.float32)
        for part in range(pl.cdiv(blocks, per)):
            if part * per + j < blocks:
                begin = 2 * edge * part
                turned = pltpu.roll(load(part * per + j), edge + begin, 1)
                acc = jnp.where((lane >= begin) & (lane < begin + 2 * edge), turned, acc)
        dst_ref[at + (slice(row + 8 * j, row + 8 * j + 8), slice(None))] = acc


def unpack(src_ref, dst_ref, skip, height, edge):
    tall = dst_ref.shape[1]
    begin = GUARD + skip
    for i in range(2):
        dst_ref[i, 0:begin, :] = jnp.zeros((begin, LANES), jnp.float32)
        dst_ref[i, begin + height :, :] = jnp.zeros((tall - begin - height, LANES), jnp.float32)
    dst_ref[0, begin : begin + height, :] = src_ref[0:height, :]
    blocks = height // 8
    per = parts_of(blocks, edge)
    for part in range(pl.cdiv(blocks, per)):
        count = 8 * min(per, blocks - part * per)
        turned = pltpu.roll(src_ref[height : height + count, :], (-(2 * part + 1) * edge) % LANES, 1)
        dst_ref[1, begin + 8 * per * part : begin + 8 * per * part + count, :] = turned


def guard(ref):
    tall = ref.shape[1]
    for i in range(2):
        ref[i, 0:GUARD, :] = jnp.zeros((GUARD, LANES), jnp.float32)
        ref[i, tall - GUARD :, :] = jnp.zeros((GUARD, LANES), jnp.float32)


def ring_member():
    member = (lax.axis_index("tm") + 1) % lax.axis_size("tm")
    return member % RING, member < RING


def coarse_coefs(own_ref, row):
    return rows_of(own_ref, (3, 4, 5), 2, row, SUB)


def defect_kernel(distance, in_ref, own_ref, d_ref, p_ref, x_ref, y_ref):
    frame = x_ref.shape[1] - 2 * GUARD
    unpack(in_ref, x_ref, 0, frame, EDGE)
    guard(y_ref)
    guard(p_ref)
    for step in range(STEPS):
        src, dst = (x_ref, y_ref) if step % 2 == 0 else (y_ref, x_ref)
        dst = p_ref if step == STEPS - 1 else dst

        def body(row, step=step, src=src, dst=dst):
            out, old = stepped(src, (), row, rows_of(own_ref, (0, 1, 2), 2, row, SUB))
            for i in range(2):
                dst[i, pl.ds(row, SUB), :] = out[i]
                if step == 0:
                    d_ref[i, pl.ds(row, SUB), :] = STEPS * out[i] - (STEPS - 1.0) * old[i]
                if step == STEPS - 1:
                    d_ref[i, pl.ds(row, SUB), :] = out[i] - d_ref[i, pl.ds(row, SUB), :]

        each_block(GUARD, GUARD + frame, body, MARCH)
    member, first = ring_member()

    @pl.when(first & ((member - distance + RING) % RING == 1))
    def _():
        unpack(in_ref, p_ref, 0, frame, EDGE)


def chain_step(src_ref, dst_ref, own_ref, d_ref, which, frame):
    def body(row):
        out, _ = stepped(src_ref, (), row, coarse_coefs(own_ref, row))
        for i in range(2):
            dst_ref[i, pl.ds(row, SUB), :] = out[i] + d_ref[which, i, pl.ds(row, SUB), :]

    each_block(GUARD, GUARD + frame, body, CHAIN)


def later_kernel(own_ref, *refs):
    (d_refs, p_refs), (all_ref, one_ref, sent_ref, x_ref, y_ref) = (refs[:RING], refs[RING : 2 * RING]), refs[2 * RING :]
    frame = x_ref.shape[1] - 2 * GUARD
    member, first = ring_member()
    begin = jnp.where(first, 1, 0)
    for at, distance in enumerate((0,) + SENDS):
        field = (member - distance + RING) % RING
        all_ref[field] = d_refs[at][...]

        @pl.when(field == GROUP)
        def _(at=at):
            x_ref[...] = p_refs[at][...]

        @pl.when(field == begin)
        def _(at=at):
            one_ref[...] = p_refs[at][...]

    guard(y_ref)
    chain_step(x_ref, y_ref, own_ref, all_ref, GROUP + 1, frame)
    chain_step(y_ref, x_ref, own_ref, all_ref, GROUP + 2, frame)
    chain_step(x_ref, y_ref, own_ref, all_ref, GROUP + 3, frame)
    at = GUARD + SKIP
    height = frame - 2 * SKIP
    sent_ref[0:height, :] = y_ref[0, at : at + height, :]
    pack_edges(lambda b: y_ref[1, at + 8 * b : at + 8 * b + 8, :], height // 8, NEAR, sent_ref, (), height)


def emit(src_ref, out_ref, field, strip):
    z = lax.axis_index("tm") % RING
    slot = (field + 1 - z + RING) % RING
    begin = GUARD + FRAME - TAIL
    out_ref[slot] = src_ref[0, begin : begin + strip + 2 * TAIL, :]


def earlier_kernel(own_ref, d_ref, one_ref, out_ref, x_ref, y_ref):
    frame = x_ref.shape[1] - 2 * GUARD
    strip = frame - 2 * FRAME
    guard(x_ref)
    guard(y_ref)
    chain_step(one_ref, y_ref, own_ref, d_ref, 1, frame)
    chain_step(y_ref, x_ref, own_ref, d_ref, 2, frame)
    chain_step(x_ref, y_ref, own_ref, d_ref, 3, frame)
    for i in range(GROUP):
        src, dst = (y_ref, x_ref) if i % 2 == 0 else (x_ref, y_ref)
        chain_step(src, dst, own_ref, d_ref, GROUP + i, frame)
        emit(dst, out_ref, GROUP + i, strip)


def last_kernel(got_ref, own_ref, d_ref, one_ref, half_ref, out_ref, x_ref, y_ref):
    frame = x_ref.shape[1] - 2 * GUARD
    strip = frame - 2 * FRAME
    unpack(got_ref, x_ref, SKIP, frame - 2 * SKIP, NEAR)
    guard(y_ref)
    out_ref[...] = half_ref[...]
    _, first = ring_member()
    for i in range(GROUP):
        src, dst = (x_ref, y_ref) if i % 2 == 0 else (y_ref, x_ref)
        chain_step(src, dst, own_ref, d_ref, i, frame)
        if i == 0:

            @pl.when(first)
            def _():
                dst[...] = one_ref[...]

        emit(dst, out_ref, i, strip)


def fine_kernel(g_ref, c_ref, lo_ref, hi_ref, *refs):
    blocks, (points_ref, last_ref, u_ref, w_ref) = refs[:RING], refs[RING:]
    rows, columns = g_ref.shape
    tiles = columns // LANES
    tall = rows + 2 * TAIL
    zero8 = jnp.zeros((GUARD, LANES), jnp.float32)
    me = lax.axis_index("tm")
    for ref in (u_ref, w_ref):
        for t in range(tiles):
            ref[t, 0:GUARD, :] = zero8
            ref[t, GUARD + tall : tall + 2 * GUARD, :] = zero8
    inner = GUARD + TAIL

    def put_u(t, row, value):
        u_ref[t, row : row + value.shape[0], :] = value

    @pl.when(me == 0)
    def _():
        spread(put_u, lo_ref, g_ref, hi_ref, 0, TAIL, GUARD)

    @pl.when(me > 0)
    def _():
        for block, distance in zip(blocks, ORDER):
            chunk = (me - distance + 1 + RING) % RING
            u_ref[chunk, GUARD : GUARD + tall, :] = block[...]

    for t in range(tiles):
        points_ref[:, t * LANES : (t + 1) * LANES] = u_ref[t, inner : inner + rows, :]
    for step in range(STEPS - 1):
        src, dst = (u_ref, w_ref) if step % 2 == 0 else (w_ref, u_ref)

        def body(row, src=src, dst=dst):
            out, _ = stepped(src, (), row, rows_of(c_ref, (0, 1, 2), tiles, row, SUB), ring=False)
            for t in range(tiles):
                dst[t, pl.ds(row, SUB), :] = out[t]

        each_block(GUARD, GUARD + tall, body, FINE)
    for t in range(tiles):
        last_ref[:, t * LANES : (t + 1) * LANES] = w_ref[t, inner : inner + rows, :]


def call(kernel, outs, scratch, cost, *args):
    flops, moved = cost
    vmem = pl.BlockSpec(memory_space=pltpu.VMEM)
    return pl.pallas_call(
        kernel,
        out_shape=[jax.ShapeDtypeStruct(s, jnp.float32) for s in outs],
        in_specs=[vmem] * len(args),
        out_specs=[vmem] * len(outs),
        scratch_shapes=[pltpu.VMEM(s, jnp.float32) for s in scratch],
        cost_estimate=pl.CostEstimate(flops=flops, bytes_accessed=moved, transcendentals=0),
        compiler_params=pltpu.CompilerParams(vmem_limit_bytes=24 << 20),
    )(*args)


def local(guess, kappa, rate):
    intervals, strips = lax.axis_size("tm"), lax.axis_size("space")
    state = guess[0]
    rows, columns = state.shape
    tiles = columns // LANES
    edges = jnp.stack([state, kappa, rate])
    up = [(i, i + 1) for i in range(strips - 1)]
    down = [(i + 1, i) for i in range(strips - 1)]
    lo = lax.ppermute(edges[:, rows - HALO :], "space", up)
    hi = lax.ppermute(edges[:, :HALO], "space", down)

    frame = rows + 2 * FRAME
    ext = rows + 2 * HALO + 2 * GUARD
    wide = frame + 2 * GUARD
    pair = (2, wide, LANES)
    height = frame - 2 * SKIP
    tall = rows + 2 * TAIL
    (packed,) = call(
        relax_kernel,
        [(RING, frame + 8 * parts_of(frame // 8, EDGE), LANES)],
        [(tiles + 1, ext, LANES), (tiles, ext, LANES), (3, tiles, ext, LANES)],
        (40 * rows * columns, 16 * rows * columns),
        state, kappa, rate, lo, hi,
    )
    own, fine = call(
        coef_kernel,
        [(6, 2, wide, LANES), (3, tiles, tall + 2 * GUARD, LANES)],
        [(3, tiles + 1, ext, LANES)],
        (DEFECT_FLOPS, rows * columns),
        kappa, rate, lo, hi, packed[0],
    )
    phis = [None] * RING
    for distance in (0,) + SENDS:
        block = packed[distance]
        if distance:
            block = lax.ppermute(block, "tm", [
                ((RING * m + i - 1) % intervals, (RING * m + (i + distance) % RING - 1) % intervals)
                for m in range(intervals // RING) for i in range(RING)
            ])
        phis[distance] = call(
            functools.partial(defect_kernel, distance), [pair, pair], [pair, pair],
            (DEFECT_FLOPS, rows * columns), block, own,
        )
    every, one, sent = call(
        later_kernel,
        [(RING,) + pair, pair, (height + 8 * parts_of(height // 8, NEAR), LANES)], [pair, pair],
        (4 * rows * columns, 4 * rows * columns), own, *(phis[at][0] for at in (0,) + SENDS), *(phis[at][1] for at in (0,) + SENDS),
    )
    got = lax.ppermute(sent, "tm", [(i, i + RING) for i in range(intervals - RING)]
                       + [(intervals - RING + i, i) for i in range(RING)])
    (half,) = call(
        earlier_kernel, [(RING, tall, LANES)], [pair, pair],
        (8 * rows * columns, 4 * rows * columns), own, every, one,
    )
    (out,) = call(
        last_kernel, [(RING, tall, LANES)], [pair, pair],
        (4 * rows * columns, 4 * rows * columns), got, own, every, one, half,
    )
    blocks = [None] * RING
    for distance in ORDER:
        pairs = []
        for m in range(intervals // RING):
            for i in range(RING):
                source = (RING * m + i - 1) % intervals
                field = (source + distance - 1) % RING
                pairs.append((source, (RING * m + 1 + field) % intervals))
        blocks[distance] = lax.ppermute(out[distance], "tm", pairs)
    c_points, last_fine = call(
        fine_kernel, [(rows, columns)] * 2,
        [(tiles, tall + 2 * GUARD, LANES)] * 2,
        (30 * rows * columns, 16 * rows * columns),
        state, fine, lo, hi, *(blocks[distance] for distance in ORDER),
    )
    return c_points[None], last_fine[None]


def solution(mesh):
    return jax.shard_map(
        local,
        mesh=mesh,
        in_specs=(P("tm", "space", None), P("space", None), P("space", None)),
        out_specs=(P("tm", "space", None), P("tm", "space", None)),
        check_vma=False,
    )
```

```python
import functools

import jax
import jax.numpy as jnp
from jax import lax
from jax.experimental import pallas as pl
from jax.experimental.pallas import tpu as pltpu
from jax.sharding import PartitionSpec as P

STEPS = 4
GROUP = 4
DIFFUSION = 0.05
RING = 8
HALO = 24
LANES = 128
FRAME = 16
EDGE = 11
SKIP, NEAR = 8, 4
TAIL = 4
GUARD = 8
SENDS = (7, 1, 6, 2, 4, 5, 3)
ORDER = (0, 1, 7, 2, 6, 4, 5, 3)
RELAX = (288,16)
SUB = 8
MARCH, CHAIN, FINE = 288, 288, 88
DEFECT_FLOPS = 20_000_000


def lane_index(height=8):
    return lax.broadcasted_iota(jnp.int32, (height, LANES), 1)


def neighbour_sum(tiles, up, down, ring):
    lane = lane_index(tiles[0].shape[0])
    count = len(tiles)
    right_turned = [pltpu.roll(t, 1, 1) for t in tiles]
    left_turned = [pltpu.roll(t, LANES - 1, 1) for t in tiles]
    sums = []
    for i in range(count):
        before = right_turned[i - 1] if ring or i > 0 else 0.0
        after = left_turned[(i + 1) % count] if ring or i + 1 < count else 0.0
        left = jnp.where(lane == 0, before, right_turned[i])
        right = jnp.where(lane == LANES - 1, after, left_turned[i])
        sums.append((up[i] + down[i]) + (left + right))
    return sums


def stepped(ref, at, row, coefs, ring=True):
    count, height = len(coefs), coefs[0][0].shape[0]
    tiles = [ref[at + (i, pl.ds(row, height), slice(None))] for i in range(count)]
    up = [ref[at + (i, pl.ds(row - 1, height), slice(None))] for i in range(count)]
    down = [ref[at + (i, pl.ds(row + 1, height), slice(None))] for i in range(count)]
    sums = neighbour_sum(tiles, up, down, ring)
    out = [k * s + c * (m - r * (c * c)) for c, s, (k, r, m) in zip(tiles, sums, coefs)]
    return out, tiles


def rows_of(ref, kinds, count, row, height):
    return [tuple(ref[k, i, pl.ds(row, height), :] for k in kinds) for i in range(count)]


def each_block(first, last, body, height):
    assert (last - first) % height == 0

    def trip(i, carry):
        row = pl.multiple_of(first + height * i, 8)
        for part in range(0, height, SUB):
            body(row + part)
        return carry

    lax.fori_loop(0, (last - first) // height, trip, 0)


def spread(put, lo_ref, body_ref, hi_ref, part, take, at):
    rows, columns = body_ref.shape
    for t in range(columns // LANES):
        cols = slice(t * LANES, (t + 1) * LANES)
        put(t, at, lo_ref[part, HALO - take : HALO, cols])
        put(t, at + take, body_ref[:, cols])
        put(t, at + take + rows, hi_ref[part, 0:take, cols])


def spread_coefs(c_ref, k_ref, r_ref, lo_ref, hi_ref, take, at):
    def put_k(t, row, value):
        c_ref[0, t, row : row + value.shape[0], :] = DIFFUSION * value

    def put_r(t, row, value):
        rows = slice(row, row + value.shape[0])
        c_ref[1, t, rows, :] = value
        c_ref[2, t, rows, :] = 1.0 - 4.0 * c_ref[0, t, rows, :] + value

    spread(put_k, lo_ref, k_ref, hi_ref, 1, take, at)
    spread(put_r, lo_ref, r_ref, hi_ref, 2, take, at)


def relax_kernel(g_ref, k_ref, r_ref, lo_ref, hi_ref, packed_ref, u_ref, w_ref, c_ref):
    rows, columns = g_ref.shape
    tiles = columns // LANES
    ext = rows + 2 * HALO
    top = GUARD + HALO
    zero8 = jnp.zeros((GUARD, LANES), jnp.float32)

    def put_u(t, row, value):
        u_ref[t, row : row + value.shape[0], :] = value

    spread(put_u, lo_ref, g_ref, hi_ref, 0, HALO, GUARD)
    spread_coefs(c_ref, k_ref, r_ref, lo_ref, hi_ref, HALO, GUARD)
    u_ref[tiles] = jnp.zeros((ext + 2 * GUARD, LANES), jnp.float32)
    for t in range(tiles):
        for ref in (u_ref, w_ref):
            ref[t, 0:GUARD, :] = zero8
            ref[t, GUARD + ext : ext + 2 * GUARD, :] = zero8

    def march(src, dst, first, last):
        height = next(h for h in RELAX if (last - first) % h == 0)

        def body(row):
            out, _ = stepped(src, (), row, rows_of(c_ref, (0, 1, 2), tiles, row, SUB), ring=False)
            for t in range(tiles):
                dst[t, pl.ds(row, SUB), :] = out[t]

        each_block(first, last, body, height)

    march(u_ref, w_ref, GUARD, GUARD + ext - 16)
    march(u_ref, w_ref, GUARD + ext - 16, GUARD + ext)
    march(w_ref, u_ref, GUARD + 8, GUARD + ext - 8)
    march(u_ref, w_ref, GUARD + 8, GUARD + ext - 8)
    march(w_ref, u_ref, GUARD + 8, GUARD + ext - 8)

    frame = rows + 2 * FRAME
    base = top - FRAME
    lane = lane_index()
    member = (lax.axis_index("tm") + 1) % RING
    for distance in range(RING):
        c = (member + distance) % RING
        after, before = c + 1, lax.rem(c + tiles, tiles + 1)
        packed_ref[distance, 0:frame, :] = u_ref[c, base : base + frame, :]

        def edge(block, after=after, before=before):
            at = base + 8 * block
            return jnp.where(lane < LANES // 2, u_ref[after, at : at + 8, :], u_ref[before, at : at + 8, :])

        pack_edges(edge, frame // 8, EDGE, packed_ref, (distance,), frame)


def coef_kernel(k_ref, r_ref, lo_ref, hi_ref, after_ref, own_ref, fine_ref, c_ref):
    del after_ref
    rows, columns = k_ref.shape
    tiles = columns // LANES
    ext = rows + 2 * HALO
    top = GUARD + HALO
    frame, tall = rows + 2 * FRAME, rows + 2 * TAIL
    base = top - FRAME
    lane = lane_index()
    zero8 = jnp.zeros((GUARD, LANES), jnp.float32)
    spread_coefs(c_ref, k_ref, r_ref, lo_ref, hi_ref, HALO, GUARD)
    pad = jnp.zeros((ext + 2 * GUARD, LANES), jnp.float32)
    for kind in range(3):
        c_ref[kind, tiles] = pad + (1.0 if kind == 2 else 0.0)
        for t in range(tiles):
            fine_ref[kind, t, 0:GUARD, :] = zero8
            fine_ref[kind, t, GUARD + tall :, :] = zero8
            fine_ref[kind, t, GUARD : GUARD + tall, :] = c_ref[kind, t, top - TAIL : top - TAIL + tall, :]
    mine = (lax.axis_index("tm") + 1) % RING
    after, before = mine + 1, lax.rem(mine + tiles, tiles + 1)
    near = (lane < EDGE) | (lane >= LANES - EDGE)
    for kind in range(3):
        own_ref[kind, 0, 0:GUARD, :] = zero8
        own_ref[kind, 1, 0:GUARD, :] = zero8
        own_ref[kind, 0, GUARD + frame :, :] = zero8
        own_ref[kind, 1, GUARD + frame :, :] = zero8

        def body(row, kind=kind):
            src = row + base - GUARD
            own_ref[kind, 0, pl.ds(row, 8), :] = c_ref[kind, mine, pl.ds(src, 8), :]
            edge = jnp.where(
                lane < LANES // 2,
                c_ref[kind, after, pl.ds(src, 8), :],
                c_ref[kind, before, pl.ds(src, 8), :],
            )
            far = 1.0 if kind == 2 else 0.0
            edge = jnp.where(near, edge, far)
            own_ref[kind, 1, pl.ds(row, 8), :] = edge
            less = STEPS - 1.0 if kind == 2 else 0.0
            own_ref[kind + 3, 0, pl.ds(row, 8), :] = STEPS * c_ref[kind, mine, pl.ds(src, 8), :] - less
            own_ref[kind + 3, 1, pl.ds(row, 8), :] = STEPS * edge - less

        each_block(GUARD, GUARD + frame, body, 8)


def parts_of(blocks, edge):
    return pl.cdiv(blocks, LANES // (2 * edge))


def pack_edges(load, blocks, edge, dst_ref, at, row):
    lane = lane_index()
    per = parts_of(blocks, edge)
    for j in range(per):
        acc = jnp.zeros((8, LANES), jnp.float32)
        for part in range(pl.cdiv(blocks, per)):
            if part * per + j < blocks:
                begin = 2 * edge * part
                turned = pltpu.roll(load(part * per + j), edge + begin, 1)
                acc = jnp.where((lane >= begin) & (lane < begin + 2 * edge), turned, acc)
        dst_ref[at + (slice(row + 8 * j, row + 8 * j + 8), slice(None))] = acc


def unpack(src_ref, dst_ref, skip, height, edge):
    tall = dst_ref.shape[1]
    begin = GUARD + skip
    for i in range(2):
        dst_ref[i, 0:begin, :] = jnp.zeros((begin, LANES), jnp.float32)
        dst_ref[i, begin + height :, :] = jnp.zeros((tall - begin - height, LANES), jnp.float32)
    dst_ref[0, begin : begin + height, :] = src_ref[0:height, :]
    blocks = height // 8
    per = parts_of(blocks, edge)
    for part in range(pl.cdiv(blocks, per)):
        count = 8 * min(per, blocks - part * per)
        turned = pltpu.roll(src_ref[height : height + count, :], (-(2 * part + 1) * edge) % LANES, 1)
        dst_ref[1, begin + 8 * per * part : begin + 8 * per * part + count, :] = turned


def guard(ref):
    tall = ref.shape[1]
    for i in range(2):
        ref[i, 0:GUARD, :] = jnp.zeros((GUARD, LANES), jnp.float32)
        ref[i, tall - GUARD :, :] = jnp.zeros((GUARD, LANES), jnp.float32)


def ring_member():
    member = (lax.axis_index("tm") + 1) % lax.axis_size("tm")
    return member % RING, member < RING


def coarse_coefs(own_ref, row):
    return rows_of(own_ref, (3, 4, 5), 2, row, SUB)


def defect_kernel(distance, in_ref, own_ref, d_ref, p_ref, x_ref, y_ref):
    frame = x_ref.shape[1] - 2 * GUARD
    unpack(in_ref, x_ref, 0, frame, EDGE)
    guard(y_ref)
    guard(p_ref)
    for step in range(STEPS):
        src, dst = (x_ref, y_ref) if step % 2 == 0 else (y_ref, x_ref)
        dst = p_ref if step == STEPS - 1 else dst

        def body(row, step=step, src=src, dst=dst):
            out, old = stepped(src, (), row, rows_of(own_ref, (0, 1, 2), 2, row, SUB))
            for i in range(2):
                dst[i, pl.ds(row, SUB), :] = out[i]
                if step == 0:
                    d_ref[i, pl.ds(row, SUB), :] = STEPS * out[i] - (STEPS - 1.0) * old[i]
                if step == STEPS - 1:
                    d_ref[i, pl.ds(row, SUB), :] = out[i] - d_ref[i, pl.ds(row, SUB), :]

        each_block(GUARD, GUARD + frame, body, MARCH)
    member, first = ring_member()

    @pl.when(first & ((member - distance + RING) % RING == 1))
    def _():
        unpack(in_ref, p_ref, 0, frame, EDGE)


def chain_step(src_ref, dst_ref, own_ref, d_ref, which, frame):
    def body(row):
        out, _ = stepped(src_ref, (), row, coarse_coefs(own_ref, row))
        for i in range(2):
            dst_ref[i, pl.ds(row, SUB), :] = out[i] + d_ref[which, i, pl.ds(row, SUB), :]

    each_block(GUARD, GUARD + frame, body, CHAIN)


def later_kernel(own_ref, *refs):
    (d_refs, p_refs), (all_ref, one_ref, sent_ref, x_ref, y_ref) = (refs[:RING], refs[RING : 2 * RING]), refs[2 * RING :]
    frame = x_ref.shape[1] - 2 * GUARD
    member, first = ring_member()
    begin = jnp.where(first, 1, 0)
    for at, distance in enumerate((0,) + SENDS):
        field = (member - distance + RING) % RING
        all_ref[field] = d_refs[at][...]

        @pl.when(field == GROUP)
        def _(at=at):
            x_ref[...] = p_refs[at][...]

        @pl.when(field == begin)
        def _(at=at):
            one_ref[...] = p_refs[at][...]

    guard(y_ref)
    chain_step(x_ref, y_ref, own_ref, all_ref, GROUP + 1, frame)
    chain_step(y_ref, x_ref, own_ref, all_ref, GROUP + 2, frame)
    chain_step(x_ref, y_ref, own_ref, all_ref, GROUP + 3, frame)
    at = GUARD + SKIP
    height = frame - 2 * SKIP
    sent_ref[0:height, :] = y_ref[0, at : at + height, :]
    pack_edges(lambda b: y_ref[1, at + 8 * b : at + 8 * b + 8, :], height // 8, NEAR, sent_ref, (), height)


def emit(src_ref, out_ref, field, strip):
    z = lax.axis_index("tm") % RING
    slot = (field + 1 - z + RING) % RING
    begin = GUARD + FRAME - TAIL
    out_ref[slot] = src_ref[0, begin : begin + strip + 2 * TAIL, :]


def earlier_kernel(own_ref, d_ref, one_ref, out_ref, x_ref, y_ref):
    frame = x_ref.shape[1] - 2 * GUARD
    strip = frame - 2 * FRAME
    guard(x_ref)
    guard(y_ref)
    chain_step(one_ref, y_ref, own_ref, d_ref, 1, frame)
    chain_step(y_ref, x_ref, own_ref, d_ref, 2, frame)
    chain_step(x_ref, y_ref, own_ref, d_ref, 3, frame)
    for i in range(GROUP):
        src, dst = (y_ref, x_ref) if i % 2 == 0 else (x_ref, y_ref)
        chain_step(src, dst, own_ref, d_ref, GROUP + i, frame)
        emit(dst, out_ref, GROUP + i, strip)


def last_kernel(got_ref, own_ref, d_ref, one_ref, half_ref, out_ref, x_ref, y_ref):
    frame = x_ref.shape[1] - 2 * GUARD
    strip = frame - 2 * FRAME
    unpack(got_ref, x_ref, SKIP, frame - 2 * SKIP, NEAR)
    guard(y_ref)
    out_ref[...] = half_ref[...]
    _, first = ring_member()
    for i in range(GROUP):
        src, dst = (x_ref, y_ref) if i % 2 == 0 else (y_ref, x_ref)
        chain_step(src, dst, own_ref, d_ref, i, frame)
        if i == 0:

            @pl.when(first)
            def _():
                dst[...] = one_ref[...]

        emit(dst, out_ref, i, strip)


def fine_kernel(g_ref, c_ref, lo_ref, hi_ref, *refs):
    blocks, (points_ref, last_ref, u_ref, w_ref) = refs[:RING], refs[RING:]
    rows, columns = g_ref.shape
    tiles = columns // LANES
    tall = rows + 2 * TAIL
    zero8 = jnp.zeros((GUARD, LANES), jnp.float32)
    me = lax.axis_index("tm")
    for ref in (u_ref, w_ref):
        for t in range(tiles):
            ref[t, 0:GUARD, :] = zero8
            ref[t, GUARD + tall : tall + 2 * GUARD, :] = zero8
    inner = GUARD + TAIL

    def put_u(t, row, value):
        u_ref[t, row : row + value.shape[0], :] = value

    @pl.when(me == 0)
    def _():
        spread(put_u, lo_ref, g_ref, hi_ref, 0, TAIL, GUARD)

    @pl.when(me > 0)
    def _():
        for block, distance in zip(blocks, ORDER):
            chunk = (me - distance + 1 + RING) % RING
            u_ref[chunk, GUARD : GUARD + tall, :] = block[...]

    for t in range(tiles):
        points_ref[:, t * LANES : (t + 1) * LANES] = u_ref[t, inner : inner + rows, :]
    for step in range(STEPS - 1):
        src, dst = (u_ref, w_ref) if step % 2 == 0 else (w_ref, u_ref)

        def body(row, src=src, dst=dst):
            out, _ = stepped(src, (), row, rows_of(c_ref, (0, 1, 2), tiles, row, SUB), ring=False)
            for t in range(tiles):
                dst[t, pl.ds(row, SUB), :] = out[t]

        each_block(GUARD, GUARD + tall, body, FINE)
    for t in range(tiles):
        last_ref[:, t * LANES : (t + 1) * LANES] = w_ref[t, inner : inner + rows, :]


def call(kernel, outs, scratch, cost, *args):
    flops, moved = cost
    vmem = pl.BlockSpec(memory_space=pltpu.VMEM)
    return pl.pallas_call(
        kernel,
        out_shape=[jax.ShapeDtypeStruct(s, jnp.float32) for s in outs],
        in_specs=[vmem] * len(args),
        out_specs=[vmem] * len(outs),
        scratch_shapes=[pltpu.VMEM(s, jnp.float32) for s in scratch],
        cost_estimate=pl.CostEstimate(flops=flops, bytes_accessed=moved, transcendentals=0),
        compiler_params=pltpu.CompilerParams(vmem_limit_bytes=24 << 20),
    )(*args)


def local(guess, kappa, rate):
    intervals, strips = lax.axis_size("tm"), lax.axis_size("space")
    state = guess[0]
    rows, columns = state.shape
    tiles = columns // LANES
    edges = jnp.stack([state, kappa, rate])
    up = [(i, i + 1) for i in range(strips - 1)]
    down = [(i + 1, i) for i in range(strips - 1)]
    lo = lax.ppermute(edges[:, rows - HALO :], "space", up)
    hi = lax.ppermute(edges[:, :HALO], "space", down)

    frame = rows + 2 * FRAME
    ext = rows + 2 * HALO + 2 * GUARD
    wide = frame + 2 * GUARD
    pair = (2, wide, LANES)
    height = frame - 2 * SKIP
    tall = rows + 2 * TAIL
    (packed,) = call(
        relax_kernel,
        [(RING, frame + 8 * parts_of(frame // 8, EDGE), LANES)],
        [(tiles + 1, ext, LANES), (tiles, ext, LANES), (3, tiles, ext, LANES)],
        (40 * rows * columns, 16 * rows * columns),
        state, kappa, rate, lo, hi,
    )
    own, fine = call(
        coef_kernel,
        [(6, 2, wide, LANES), (3, tiles, tall + 2 * GUARD, LANES)],
        [(3, tiles + 1, ext, LANES)],
        (DEFECT_FLOPS, rows * columns),
        kappa, rate, lo, hi, packed[0],
    )
    phis = [None] * RING
    for distance in (0,) + SENDS:
        block = packed[distance]
        if distance:
            block = lax.ppermute(block, "tm", [
                ((RING * m + i - 1) % intervals, (RING * m + (i + distance) % RING - 1) % intervals)
                for m in range(intervals // RING) for i in range(RING)
            ])
        phis[distance] = call(
            functools.partial(defect_kernel, distance), [pair, pair], [pair, pair],
            (DEFECT_FLOPS, rows * columns), block, own,
        )
    every, one, sent = call(
        later_kernel,
        [(RING,) + pair, pair, (height + 8 * parts_of(height // 8, NEAR), LANES)], [pair, pair],
        (4 * rows * columns, 4 * rows * columns), own, *(phis[at][0] for at in (0,) + SENDS), *(phis[at][1] for at in (0,) + SENDS),
    )
    got = lax.ppermute(sent, "tm", [(i, i + RING) for i in range(intervals - RING)]
                       + [(intervals - RING + i, i) for i in range(RING)])
    (half,) = call(
        earlier_kernel, [(RING, tall, LANES)], [pair, pair],
        (8 * rows * columns, 4 * rows * columns), own, every, one,
    )
    (out,) = call(
        last_kernel, [(RING, tall, LANES)], [pair, pair],
        (4 * rows * columns, 4 * rows * columns), got, own, every, one, half,
    )
    blocks = [None] * RING
    for distance in ORDER:
        pairs = []
        for m in range(intervals // RING):
            for i in range(RING):
                source = (RING * m + i - 1) % intervals
                field = (source + distance - 1) % RING
                pairs.append((source, (RING * m + 1 + field) % intervals))
        blocks[distance] = lax.ppermute(out[distance], "tm", pairs)
    c_points, last_fine = call(
        fine_kernel, [(rows, columns)] * 2,
        [(tiles, tall + 2 * GUARD, LANES)] * 2,
        (30 * rows * columns, 16 * rows * columns),
        state, fine, lo, hi, *(blocks[distance] for distance in ORDER),
    )
    return c_points[None], last_fine[None]


def solution(mesh):
    return jax.shard_map(
        local,
        mesh=mesh,
        in_specs=(P("tm", "space", None), P("space", None), P("space", None)),
        out_specs=(P("tm", "space", None), P("tm", "space", None)),
        check_vma=False,
    )
```
